256 devices in a mesh: shot: 64 (over y, x, z_hi), sub: 4 (over z_lo, core).
Axes of the slice: x: 4, y: 4, z: 8 (z_hi: 4, z_lo: 2; z = z_hi * 2 + z_lo), core: 2. Of those that a mesh axis runs over, the one named last changes fastest.
Arguments:
- q_model: float32 [256, 128, 256], P('shot', 'sub'), may hold values from 0.04 to 0.18
- tile_slot: int32 [256], replicated, may hold values from 0 to 255, as said below
- tile_list: int32 [64, 16], replicated, may hold values from 0 to 255, as said below
- rec_index: int32 [64, 256], P('shot'), may hold values from 0 to 524287
- traces: float32 [64, 8, 256], P('shot'), may hold values from -6 to 6
- adj_now: float32 [64, 128, 4096], P('shot', 'sub'), may hold values from -6 to 6
- adj_prev: float32 [64, 128, 4096], P('shot', 'sub'), may hold values from -6 to 6
- fwd_lap: bfloat16 [64, 8, 128, 4096], P('shot', None, 'sub'), may hold values from -0.59765625 to 0.59765625
Outputs:
- gradient: float32 [256, 128, 256], P('shot', 'sub')
- adj_final: bfloat16 [64, 128, 4096], P('shot', 'sub')
The draws below stay inside these ranges and needn't reach their ends.
Inputs may be any that keep to these rules, and one draw needn't show every extreme that they name: `tile_slot`: A permutation; slots 4 * i to 4 * i + 3 are those of index i of shot. `tile_list`: each row holds 16 distinct tiles. Of one row's tiles at most 2 lie in the slots of one index of shot, and exactly 2 do for some index in every row.
All inputs are finite; a program needn't handle non-finite values.
Results may differ from the reference program's by a relative error of at most 0.001.
Values sent between devices are 32-bit elements; how exact they have to be, the bound alone decides.
A program may use at most 128 MiB of HBM per device.

```python
import math
import jax
import jax.numpy as jnp
from jax import lax

TS = 16
STEPS = 8
NREC = 256
TILE_DEV = 4
AGX = 4
AGY = 4
AP = 16
NT = 256
AX = 64
AY = 64
DZ = 128
N_SHOT = 64


def routing_draw(key):
    shots = NT // TILE_DEV
    doubles = max(AP // 4, AP - shots)
    singles = AP - 2 * doubles

    def per_shot(shot_key):
        first_key, second_key, third_key = jax.random.split(shot_key, 3)
        owner_order = jax.random.permutation(first_key, shots)
        owner_rank = jnp.argsort(owner_order, stable=True)
        counts = jnp.where(owner_rank < doubles, 2, jnp.where(owner_rank < doubles + singles, 1, 0))
        slot_keys = jax.random.split(second_key, shots)
        order = jax.vmap(lambda inner: jax.random.permutation(inner, TILE_DEV))(slot_keys)
        slots = jnp.arange(shots)[:, None] * TILE_DEV + order
        used = (jnp.arange(TILE_DEV)[None, :] < counts[:, None]).astype(jnp.int32)
        flat_used = used.reshape(-1)
        flat_slots = slots.reshape(-1)
        first = jnp.argsort(1 - flat_used, stable=True)[:AP]
        chosen = flat_slots[first]
        return chosen[jax.random.permutation(third_key, AP)]
    slot_to_tile = jax.random.permutation(jax.random.fold_in(key, 1), NT)
    shot_keys = jax.random.split(jax.random.fold_in(key, 2), shots)
    chosen_slots = jax.vmap(per_shot)(shot_keys)
    lists = slot_to_tile[chosen_slots]
    tile_slot = jnp.argsort(slot_to_tile, stable=True)
    return (tile_slot.astype(jnp.int32), lists.astype(jnp.int32))


def draw_tile_slot(key, part):
    return routing_draw(jax.random.fold_in(key, 7))[0]


def draw_tile_list(key, part):
    return routing_draw(jax.random.fold_in(key, 7))[1]


def touch_ends(array, own_key, smallest, top_value):
    index_at = [jax.random.randint(jax.random.fold_in(own_key, axis), (), 0, length) for axis, length in enumerate(array.shape)]
    main_axis = array.shape.index(max(array.shape))
    neighbour = index_at[:main_axis] + [(index_at[main_axis] + 1) % array.shape[main_axis]] + index_at[main_axis + 1:]
    return array.at[tuple(index_at)].set(smallest).at[tuple(neighbour)].set(top_value)


def shard_levels(stream_key, shape, cuts, low, high):
    def one(axis_at, parts):
        draws = jax.random.uniform(jax.random.fold_in(jax.random.fold_in(stream_key, 6), axis_at), (parts,), jnp.float32, low / len(cuts), high / len(cuts))
        return jnp.repeat(jnp.exp(draws), shape[axis_at] // parts).reshape((-1,) + (1,) * (len(shape) - axis_at - 1))

    level = one(*cuts[0])
    for cut in cuts[1:]:
        level = level * one(*cut)
    return level


def bell_draw(key, shape, deviation, limit, pieces=(), held_as=jnp.bfloat16):
    values = jax.random.normal(key, shape, jnp.float32) * deviation
    if len(pieces) > 0:
        values = shard_levels(key, shape, pieces, -0.22, 0.18) * values
    return jnp.clip(values, min=-limit, max=limit).astype(held_as)


def setup_inputs(seed: int = 0) -> dict:
    keys = jax.random.split(jax.random.key(seed), 9)
    return {
        "q_model": jnp.clip(jnp.exp(math.log(0.18) - 1.50407746 * jax.random.uniform(keys[0], (NT, DZ, TS * TS), jnp.float32) ** shard_levels(keys[0], (NT, DZ, TS * TS), ((0, 64), (1, 4)), -0.2, 0.2)), 0.04, 0.18),
        "tile_slot": draw_tile_slot(jax.random.fold_in(keys[8], 71), 0),
        "tile_list": draw_tile_list(jax.random.fold_in(keys[8], 71), 0),
        "rec_index": touch_ends(jax.random.randint(keys[3], (N_SHOT, NREC), 0, AX * AY * DZ), jax.random.fold_in(keys[3], 1), 0, (AX * AY * DZ) - 1).astype(jnp.int32),
        "traces": bell_draw(keys[4], (N_SHOT, STEPS, NREC), 1.0, 6.0, ((0, 64),), jnp.float32),
        "adj_now": bell_draw(keys[5], (N_SHOT, DZ, AX * AY), 1.0, 6.0, ((0, 64), (1, 4)), jnp.float32),
        "adj_prev": bell_draw(keys[6], (N_SHOT, DZ, AX * AY), 1.0, 6.0, ((0, 64), (1, 4)), jnp.float32),
        "fwd_lap": bell_draw(keys[7], (N_SHOT, STEPS, DZ, AX * AY), 0.1, 0.59765625, ((0, 64), (2, 4))),
    }


COEFFS = (-205.0 / 72.0, 8.0 / 5.0, -1.0 / 5.0, 8.0 / 315.0, -1.0 / 560.0)


def laplace(field):
    size_a, size_b, size_c = field.shape
    padded = jnp.pad(field, 4)

    def window(shift_a, shift_b, shift_c):
        return padded[4 + shift_a:4 + shift_a + size_a, 4 + shift_b:4 + shift_b + size_b, 4 + shift_c:4 + shift_c + size_c]

    total = 3.0 * COEFFS[0] * field
    for reach in range(1, 5):
        beside_all = window(reach, 0, 0) + window(-reach, 0, 0) + window(0, reach, 0) + window(0, -reach, 0) + window(0, 0, reach) + window(0, 0, -reach)
        total = total + COEFFS[reach] * beside_all
    return total


def reference(q_model, tile_slot, tile_list, rec_index, traces, adj_now, adj_prev, fwd_lap):
    ntiles = q_model.shape[0]
    depth = q_model.shape[1]
    cells = depth * TS * TS
    flat_model = q_model.reshape(ntiles, cells)

    def one_shot(total, shot_row):
        slots = tile_slot[tile_list[shot_row]]
        tiles = jnp.take(flat_model, slots, axis=0)
        speed = tiles.reshape(AGX, AGY, depth, TS, TS).transpose(2, 0, 3, 1, 4).reshape(depth, AX, AY)
        current = adj_now[shot_row].reshape(depth, AX, AY)
        previous = adj_prev[shot_row].reshape(depth, AX, AY)
        image = jnp.zeros((depth, AX, AY), jnp.float32)
        receivers = rec_index[shot_row]
        for step in range(STEPS):
            source = jnp.zeros((AX * AY * depth,), jnp.float32).at[receivers].add(traces[shot_row, step]).reshape(depth, AX, AY)
            updated = 2.0 * current - previous + speed * laplace(current) + source
            image = image + fwd_lap[shot_row, step].astype(jnp.float32).reshape(depth, AX, AY) * updated
            previous = current
            current = updated
        blocks = image.reshape(depth, AGX, TS, AGY, TS).transpose(1, 3, 0, 2, 4).reshape(AP, cells)
        total = total.at[slots].add(blocks)
        return total, current.reshape(depth, AX * AY).astype(jnp.bfloat16)

    start = jnp.zeros((ntiles, cells), jnp.float32)
    total, finals = lax.scan(one_shot, start, jnp.arange(N_SHOT, dtype=jnp.int32))
    return total.reshape(q_model.shape), finals
```

```python
import functools

import jax
import jax.numpy as jnp
import numpy as np
from jax import lax
from jax.experimental import pallas as pl
from jax.experimental.pallas import tpu as pltpu
from jax.sharding import PartitionSpec as P

TS = 16
STEPS = 8
ROWS = 32
LANES = 256
PLANE = 4096
COEFFS = (-205.0 / 72.0, 8.0 / 5.0, -1.0 / 5.0, 8.0 / 315.0, -1.0 / 560.0)
C1 = COEFFS[1]
REL = tuple(c / C1 for c in COEFFS)

NCH = 2
R = ROWS // NCH

MESH = pl.DeviceIdType.MESH
VMEM_LIMIT = 60 * 1024 * 1024
F32 = jnp.float32
BF16 = jnp.bfloat16


def lateral_matrices():
    out = np.zeros((3, LANES, LANES), np.float32)
    k = np.arange(LANES)[:, None]
    n = np.arange(LANES)[None, :]
    for d in (-1, 0, 1):
        dx = 4 * d + k // 64 - n // 64
        dy = k % 64 - n % 64
        for reach in range(1, 5):
            hit = ((dx == 0) & (np.abs(dy) == reach)) | ((dy == 0) & (np.abs(dx) == reach))
            out[d + 1][hit] = REL[reach]
    return out


def coords():
    me = lax.axis_index("shot")
    return me // 16, (me // 4) % 4, me % 4


def shot_at(y, x, z):
    return (y * 4 + x) * 4 + z


class Links:
    def __init__(self):
        self.y, self.x, self.z = coords()
        self.sub = lax.axis_index("sub")

    def step(self, axis, delta):
        y, x, z = self.y, self.x, self.z
        if axis == "y":
            y = (y + delta + 4) % 4
        elif axis == "x":
            x = (x + delta + 4) % 4
        else:
            z = (z + delta + 4) % 4
        return shot_at(y, x, z)

    def barrier(self):
        sem = pltpu.get_barrier_semaphore()
        for axis in ("y", "x", "z"):
            for delta in (1, -1):
                pl.semaphore_signal(
                    sem, inc=1, device_id=(self.step(axis, delta), self.sub), device_id_type=MESH
                )
        pl.semaphore_wait(sem, 6)


def ring(v):
    return (v + 8) % 4


def rcopy(links, axis, delta, src, dst, ssem, rsem, c, k):
    return pltpu.make_async_remote_copy(
        src_ref=src,
        dst_ref=dst,
        send_sem=ssem.at[c, k],
        recv_sem=rsem.at[c, k],
        device_id=(links.step(axis, delta), links.sub),
        device_id_type=MESH,
    )


def axes_of(c):
    return ("x", "y") if c % 2 == 0 else ("y", "x")


def slot_parts(slot, order):
    if order == 0:
        return slot // 64, slot % 64
    return (slot // 4) // 4 % 4, (slot // 64) * 16 + slot % 16


def gather_kernel(ts, tl, q_ref, out_ref, *scratch):
    g = scratch[:NCH]
    rel_s = scratch[NCH : 2 * NCH]
    rel_r = scratch[2 * NCH : 3 * NCH]
    blk_s = scratch[3 * NCH : 4 * NCH]
    blk_r = scratch[4 * NCH : 5 * NCH]
    ssem, rsem = scratch[5 * NCH], scratch[5 * NCH + 1]
    links = Links()
    here = {"y": links.y, "x": links.x, "z": links.z}
    z = links.z
    links.barrier()
    sent = []

    def go(copy):
        copy.start()
        sent.append(copy)
        return copy

    def rows(c):
        return pl.ds(c * R, R)

    def part(line, zz, t0=0, n=4):
        return pl.ds(line * 16 + zz * 4 + t0, n)

    p1, p2 = {}, {}
    for c in range(NCH):
        line = here[axes_of(c)[0]]
        src = q_ref.at[:, rows(c)]
        for d, delta in enumerate((1, -1)):
            p1[c, d] = go(rcopy(links, "z", delta, src, g[c].at[part(line, z)], ssem, rsem, c, d))
    for c in range(NCH):
        line = here[axes_of(c)[0]]
        for t in range(4):
            g[c][line * 16 + z * 4 + t] = q_ref[t, c * R : (c + 1) * R, :]
    for c in range(NCH):
        line = here[axes_of(c)[0]]
        for d, delta in enumerate((1, -1)):
            p1[c, d].wait_recv()
            piece = g[c].at[part(line, ring(z - delta), 2 * d, 2)]
            p2[c, d] = go(rcopy(links, "z", delta, piece, piece, ssem, rsem, c, 2 + d))
    a1, a2 = {}, {}
    for c in range(NCH):
        axis = axes_of(c)[0]
        line = here[axis]
        for d in range(2):
            p2[c, d].wait_recv()
        block = g[c].at[pl.ds(line * 16, 16)]
        for d, delta in enumerate((1, -1)):
            a1[c, d] = go(rcopy(links, axis, delta, block, block, ssem, rsem, c, 4 + d))
    for c in range(NCH):
        axis = axes_of(c)[0]
        line = here[axis]
        for d, delta in enumerate((1, -1)):
            a1[c, d].wait_recv()
            piece = g[c].at[pl.ds(ring(line - delta) * 16 + 8 * d, 8)]
            a2[c, d] = go(rcopy(links, axis, delta, piece, piece, ssem, rsem, c, 6 + d))

    def target(c, delta, p):
        last = axes_of(c)[1]
        slot = ts[tl[links.step(last, delta), p]]
        return slot_parts(slot, c % 2)

    rl, bl = {}, {}
    for c in range(NCH):
        last = axes_of(c)[1]
        for d in range(2):
            a2[c, d].wait_recv()
        for d, delta in enumerate((1, -1)):
            for p in range(8):
                _, at = target(c, 2, 8 * d + p)
                rel_s[c][d, p] = g[c][at]
            rl[c, d] = go(
                rcopy(links, last, delta, rel_s[c].at[d], rel_r[c].at[d], ssem, rsem, c, 8 + d)
            )
    for c in range(NCH):
        last = axes_of(c)[1]
        mine = here[last]
        for d, delta in enumerate((1, -1)):
            rl[c, d].wait_recv()
            for p in range(16):
                owner, at = target(c, delta, p)
                value = g[c][at]
                if p // 8 == d:
                    value = jnp.where(owner == mine, value, rel_r[c][d, p % 8])
                blk_s[c][d, p] = value
            bl[c, d] = go(
                rcopy(links, last, delta, blk_s[c].at[d], blk_r[c].at[d], ssem, rsem, c, 10 + d)
            )
    for c in range(NCH):
        mine = here[axes_of(c)[1]]
        for d in range(2):
            bl[c, d].wait_recv()
        for p in range(16):
            owner, at = target(c, 0, p)
            gap = ring(owner - mine)
            if p < 8:
                other = jnp.where(gap == 1, blk_r[c][1, p], blk_r[c][0, p])
            else:
                other = jnp.where(gap == 3, blk_r[c][0, p], blk_r[c][1, p])
            out_ref[p, c * R : (c + 1) * R, :] = jnp.where(gap == 0, g[c][at], other)
    for copy in sent:
        copy.wait_send()


def gather_tiles(tile_slot, tile_list, q_model):
    smem = pl.BlockSpec(memory_space=pltpu.SMEM)
    vmem = pl.BlockSpec(memory_space=pltpu.VMEM)
    scratch = (
        [pltpu.VMEM((64, R, LANES), F32)] * NCH
        + [pltpu.VMEM((2, 8, R, LANES), F32)] * (2 * NCH)
        + [pltpu.VMEM((2, 16, R, LANES), F32)] * (2 * NCH)
        + [pltpu.SemaphoreType.DMA((NCH, 12))] * 2
    )
    return pl.pallas_call(
        gather_kernel,
        out_shape=jax.ShapeDtypeStruct((16, ROWS, LANES), F32),
        in_specs=[smem, smem, vmem],
        out_specs=vmem,
        scratch_shapes=scratch,
        compiler_params=pltpu.CompilerParams(
            collective_id=0, has_side_effects=True, vmem_limit_bytes=VMEM_LIMIT
        ),
    )(tile_slot, tile_list, q_model)


def split2(v):
    hi = v.astype(BF16)
    return hi, (v - hi.astype(F32)).astype(BF16)


def split3(v):
    hi = v.astype(BF16)
    rest = v - hi.astype(F32)
    mid = rest.astype(BF16)
    return hi, mid, (rest - mid.astype(F32)).astype(BF16)


def dot(a, b, transposed=False):
    dims = (((1,), (1,)), ((), ())) if transposed else (((1,), (0,)), ((), ()))
    return lax.dot_general(a, b, dims, preferred_element_type=F32)


def steps_kernel(
    rec, tr, u_in, w_in, fwd, qt, mats, gt_out, fin_out,
    U, H, LO, Q, G, S, PM, T3, hs, hr, ssem, rsem,
):
    shot, sub = lax.axis_index("shot"), lax.axis_index("sub")
    has_up, has_dn = sub > 0, sub < 3
    sides = ((has_up, sub - 1), (has_dn, sub + 1))
    sem = pltpu.get_barrier_semaphore()
    for has, other in sides:

        @pl.when(has)
        def _():
            pl.semaphore_signal(sem, inc=1, device_id=(shot, other), device_id_type=MESH)

    pl.semaphore_wait(sem, has_up.astype(jnp.int32) + has_dn.astype(jnp.int32))

    def halo(slot, side, c):
        return pltpu.make_async_remote_copy(
            src_ref=hs.at[slot, side, c],
            dst_ref=hr.at[slot, 1 - side, c],
            send_sem=ssem.at[slot, side, c],
            recv_sem=rsem.at[slot, 1 - side, c],
            device_id=(shot, sides[side][1]),
            device_id_type=MESH,
        )

    def halo_in(slot, side, c):
        return pltpu.make_async_remote_copy(
            src_ref=hs.at[slot, side, c],
            dst_ref=hr.at[slot, side, c],
            send_sem=ssem.at[slot, side, c],
            recv_sem=rsem.at[slot, side, c],
            device_id=(shot, sides[side][1]),
            device_id_type=MESH,
        )

    zeros8 = jnp.zeros((32, 8, 128), F32)
    for par in range(2):
        U[par, :, 0:8, :] = zeros8
        U[par, :, 40:48, :] = zeros8
        for buf in (H, LO):
            buf[par, 0:32, :] = jnp.zeros((32, LANES), BF16)
            buf[par, 544:576, :] = jnp.zeros((32, LANES), BF16)
    for c in range(4):
        for k in range(8):
            cb = 8 * c + k
            value = u_in[0, :, cb * 128 : (cb + 1) * 128]
            U[0, cb, 8:40, :] = value
            hs[0, 0, c, k] = value[0:4]
            hs[0, 1, c, k] = value[28:32]
            U[1, cb, 8:40, :] = w_in[0, :, cb * 128 : (cb + 1) * 128]
        for side in range(2):

            @pl.when(sides[side][0])
            def _():
                halo(0, side, c).start()

    for j in range(16):
        hi, lo = split2(u_in[0, :, j * LANES : (j + 1) * LANES])
        H[0, 32 + 32 * j : 64 + 32 * j, :] = hi
        LO[0, 32 + 32 * j : 64 + 32 * j, :] = lo
    G[...] = jnp.zeros(G.shape, F32)

    receivers = rec[...]
    column = receivers & (PLANE - 1)
    level = (receivers >> 12) - sub * ROWS
    depth_at = lax.broadcasted_iota(jnp.int32, (ROWS, LANES), 0)
    at_depth = depth_at == level
    for t in range(STEPS):
        value = jnp.where(at_depth, tr[0, t : t + 1, :], 0.0)
        for s, v in enumerate(split3(value)):
            T3[s, 32 * t : 32 * t + 32, 0:LANES] = v
    cell = lax.broadcasted_iota(jnp.int32, (LANES, LANES), 0)

    def source_block(j, carry):
        onehot = (cell + j * LANES == column).astype(F32).astype(BF16)
        total = dot(T3[0, :, 0:LANES], onehot, True)
        total = total + dot(T3[1, :, 0:LANES], onehot, True)
        total = total + dot(T3[2, :, 0:LANES], onehot, True)
        for t in range(STEPS):
            S[t, j] = total[32 * t : 32 * t + 32]
        return carry

    lax.fori_loop(0, 16, source_block, 0)

    src = lax.broadcasted_iota(jnp.int32, (512, 512), 0)
    dst = lax.broadcasted_iota(jnp.int32, (512, 512), 1)
    moved = ((src >> 4) & 7) * 64 + (src >> 7) * 16 + (src & 15)
    PM[...] = (moved == dst).astype(F32).astype(BF16)

    for a in range(4):
        for h in range(2):
            row = 32 * (2 * a + h)
            wide = jnp.concatenate(
                [qt[4 * a + b, :, 128 * h : 128 * h + 128] for b in range(4)], axis=1
            )
            for s, v in enumerate(split3(wide * C1)):
                T3[s, row : row + 32, :] = v
    for n in range(2):
        perm = PM[:, LANES * n : LANES * n + LANES]
        total = dot(T3[0], perm) + dot(T3[1], perm) + dot(T3[2], perm)
        for k in range(8):
            Q[2 * k + n] = total[32 * k : 32 * k + 32]

    def one_step(t, carry):
        par = lax.rem(t, 2)
        nxt = 1 - par
        for c in range(4):
            for side in range(2):

                @pl.when(sides[side][0])
                def _():
                    halo(par, side, c).wait_send()
                    halo_in(par, side, c).wait_recv()
                    first = 4 if side == 0 else 40
                    for k in range(8):
                        U[par, 8 * c + k, first : first + 4, :] = hr[par, side, c, k]

            lateral = None
            for d in range(3):
                rows = pl.ds(128 * c + 32 * d, 128)
                for buf in (H, LO):
                    term = dot(buf[par, rows, :], mats[d])
                    lateral = term if lateral is None else lateral + term
            for jj in range(4):
                j = 4 * c + jj
                half = []
                for h in range(2):
                    cb = 2 * j + h
                    here = U[par, cb, 8:40, :]
                    acc = (3.0 * REL[0]) * here
                    for reach in range(1, 5):
                        beside = U[par, cb, 8 + reach : 40 + reach, :] + U[par, cb, 8 - reach : 40 - reach, :]
                        acc = acc + (beside if reach == 1 else REL[reach] * beside)
                    lanes = slice(128 * h, 128 * h + 128)
                    acc = acc + lateral[32 * jj : 32 * jj + 32, lanes]
                    new = 2.0 * here - U[nxt, cb, 8:40, :] + Q[j, :, lanes] * acc + S[t, j, :, lanes]
                    G[j, :, lanes] += fwd[0, t, :, cb * 128 : cb * 128 + 128].astype(F32) * new
                    U[nxt, cb, 8:40, :] = new
                    hs[nxt, 0, c, 2 * jj + h] = new[0:4]
                    hs[nxt, 1, c, 2 * jj + h] = new[28:32]
                    half.append(new)
                hi, lo = split2(jnp.concatenate(half, axis=1))
                H[nxt, 32 + 32 * j : 64 + 32 * j, :] = hi
                LO[nxt, 32 + 32 * j : 64 + 32 * j, :] = lo
            for side in range(2):

                @pl.when(sides[side][0] & (t < STEPS - 1))
                def _():
                    halo(nxt, side, c).start()

        return carry

    lax.fori_loop(0, STEPS, one_step, 0)

    for cb in range(32):
        fin_out[0, :, cb * 128 : (cb + 1) * 128] = U[STEPS % 2, cb, 8:40, :].astype(BF16)
    for k in range(8):
        wide = jnp.concatenate([G[2 * k], G[2 * k + 1]], axis=1)
        for s, v in enumerate(split3(wide)):
            T3[s, 32 * k : 32 * k + 32, :] = v
    for n in range(2):
        perm = PM[LANES * n : LANES * n + LANES, :]
        total = dot(T3[0], perm, True) + dot(T3[1], perm, True) + dot(T3[2], perm, True)
        for k in range(8):
            a, h = k // 2, k % 2
            for b in range(2):
                gt_out[4 * a + 2 * n + b, :, 128 * h : 128 * h + 128] = total[
                    32 * k : 32 * k + 32, 128 * b : 128 * b + 128
                ]


def time_steps(rec_index, traces, adj_now, adj_prev, fwd_lap, tiles):
    vmem = pl.BlockSpec(memory_space=pltpu.VMEM)
    mats = jnp.asarray(lateral_matrices(), BF16)
    scratch = [
        pltpu.VMEM((2, 32, 48, 128), F32),
        pltpu.VMEM((2, 576, LANES), BF16),
        pltpu.VMEM((2, 576, LANES), BF16),
        pltpu.VMEM((16, ROWS, LANES), F32),
        pltpu.VMEM((16, ROWS, LANES), F32),
        pltpu.VMEM((STEPS, 16, ROWS, LANES), F32),
        pltpu.VMEM((512, 512), BF16),
        pltpu.VMEM((3, 256, 512), BF16),
        pltpu.VMEM((2, 2, 4, 8, 4, 128), F32),
        pltpu.VMEM((2, 2, 4, 8, 4, 128), F32),
        pltpu.SemaphoreType.DMA((2, 2, 4)),
        pltpu.SemaphoreType.DMA((2, 2, 4)),
    ]
    return pl.pallas_call(
        steps_kernel,
        out_shape=(
            jax.ShapeDtypeStruct((16, ROWS, LANES), F32),
            jax.ShapeDtypeStruct((1, ROWS, PLANE), BF16),
        ),
        in_specs=[vmem] * 7,
        out_specs=(vmem, vmem),
        scratch_shapes=scratch,
        compiler_params=pltpu.CompilerParams(
            collective_id=1, has_side_effects=True, vmem_limit_bytes=VMEM_LIMIT
        ),
    )(rec_index, traces, adj_now, adj_prev, fwd_lap, tiles, mats)


def scatter_kernel(ts, tl, g16, out_ref, *scratch):
    gg = scratch[:NCH]
    rel_s = scratch[NCH : 2 * NCH]
    rel_r = scratch[2 * NCH : 3 * NCH]
    blk_s = scratch[3 * NCH : 4 * NCH]
    blk_r = scratch[4 * NCH : 5 * NCH]
    col = scratch[5 * NCH : 6 * NCH]
    zrel_r = scratch[6 * NCH : 7 * NCH]
    zblk_s = scratch[7 * NCH : 8 * NCH]
    zblk_r = scratch[8 * NCH : 9 * NCH]
    tabv, tab, ssem, rsem, lsem = scratch[9 * NCH :]
    links = Links()
    here = {"y": links.y, "x": links.x, "z": links.z}
    z = links.z
    links.barrier()
    sent = []

    def go(copy):
        copy.start()
        sent.append(copy)
        return copy

    a1, a2 = {}, {}
    for c in range(NCH):
        first = axes_of(c)[1]
        m = here[first]
        for d, delta in enumerate((1, -1)):
            a1[c, d] = go(
                rcopy(
                    links, first, delta, g16.at[:, pl.ds(c * R, R)],
                    gg[c].at[pl.ds(m * 16, 16)], ssem, rsem, c, d,
                )
            )

    row_at = lax.broadcasted_iota(jnp.int32, (8, 128), 0)
    lane_at = lax.broadcasted_iota(jnp.int32, (8, 128), 1)

    def table_row(p, acc):
        for order in range(2):
            first = ("y", "x")[order]
            m = here[first]
            for src in range(4):
                slot = ts[tl[links.step(first, src - m), p]]
                owner, at = slot_parts(slot, order)
                at = jnp.where(owner == m, at, -1)
                hit = (row_at == order * 4 + src) & (lane_at == at)
                acc = jnp.where(hit, src * 16 + p, acc)
        return acc

    tabv[...] = lax.fori_loop(0, 16, table_row, jnp.full((8, 128), 64, jnp.int32))
    fill = pltpu.make_async_copy(tabv, tab, lsem)
    fill.start()
    for c in range(NCH):
        m = here[axes_of(c)[1]]
        gg[c][64] = jnp.zeros((R, LANES), F32)
        for p in range(16):
            gg[c][m * 16 + p] = g16[p, c * R : (c + 1) * R, :]
    fill.wait()

    for c in range(NCH):
        first = axes_of(c)[1]
        m = here[first]
        for d, delta in enumerate((1, -1)):
            a1[c, d].wait_recv()
            piece = gg[c].at[pl.ds(ring(m - delta) * 16 + 8 * d, 8)]
            a2[c, d] = go(rcopy(links, first, delta, piece, piece, ssem, rsem, c, 2 + d))

    def partial(c, line, e):
        order = c % 2
        total = None
        for src in range(4):
            term = gg[c][tab[order * 4 + src, line * 16 + e]]
            total = term if total is None else total + term
        return total

    rl, bl = {}, {}
    for c in range(NCH):
        axis = axes_of(c)[0]
        line = here[axis]
        for d in range(2):
            a2[c, d].wait_recv()
        for d, delta in enumerate((1, -1)):
            for e in range(8):
                rel_s[c][d, e] = partial(c, ring(line + 2), 8 * d + e)
            rl[c, d] = go(
                rcopy(links, axis, delta, rel_s[c].at[d], rel_r[c].at[d], ssem, rsem, c, 4 + d)
            )
    for c in range(NCH):
        axis = axes_of(c)[0]
        line = here[axis]
        for d, delta in enumerate((1, -1)):
            rl[c, d].wait_recv()
            for e in range(16):
                value = partial(c, ring(line + delta), e)
                if e // 8 == d:
                    value = value + rel_r[c][d, e % 8]
                blk_s[c][d, e] = value
            bl[c, d] = go(
                rcopy(links, axis, delta, blk_s[c].at[d], blk_r[c].at[d], ssem, rsem, c, 6 + d)
            )
    zr, zb = {}, {}
    for c in range(NCH):
        line = here[axes_of(c)[0]]
        for e in range(16):
            col[c][e] = partial(c, line, e)
        for d in range(2):
            bl[c, d].wait_recv()
        for e in range(16):
            col[c][e] += blk_r[c][0, e] + blk_r[c][1, e]
        for d, delta in enumerate((1, -1)):
            zr[c, d] = go(
                rcopy(
                    links, "z", delta, col[c].at[pl.ds(ring(z + 2) * 4 + 2 * d, 2)],
                    zrel_r[c].at[d], ssem, rsem, c, 8 + d,
                )
            )
    for c in range(NCH):
        for d, delta in enumerate((1, -1)):
            zr[c, d].wait_recv()
            for t in range(4):
                value = col[c][ring(z + delta) * 4 + t]
                if t // 2 == d:
                    value = value + zrel_r[c][d, t % 2]
                zblk_s[c][d, t] = value
            zb[c, d] = go(
                rcopy(links, "z", delta, zblk_s[c].at[d], zblk_r[c].at[d], ssem, rsem, c, 10 + d)
            )
    for c in range(NCH):
        for d in range(2):
            zb[c, d].wait_recv()
        for t in range(4):
            out_ref[t, c * R : (c + 1) * R, :] = col[c][z * 4 + t] + zblk_r[c][0, t] + zblk_r[c][1, t]
    for copy in sent:
        copy.wait_send()


def scatter_tiles(tile_slot, tile_list, grad):
    smem = pl.BlockSpec(memory_space=pltpu.SMEM)
    vmem = pl.BlockSpec(memory_space=pltpu.VMEM)
    scratch = (
        [pltpu.VMEM((65, R, LANES), F32)] * NCH
        + [pltpu.VMEM((2, 8, R, LANES), F32)] * (2 * NCH)
        + [pltpu.VMEM((2, 16, R, LANES), F32)] * (2 * NCH)
        + [pltpu.VMEM((16, R, LANES), F32)] * NCH
        + [pltpu.VMEM((2, 2, R, LANES), F32)] * NCH
        + [pltpu.VMEM((2, 4, R, LANES), F32)] * (2 * NCH)
        + [pltpu.VMEM((8, 128), jnp.int32), pltpu.SMEM((8, 128), jnp.int32)]
        + [pltpu.SemaphoreType.DMA((NCH, 12))] * 2
        + [pltpu.SemaphoreType.DMA]
    )
    return pl.pallas_call(
        scatter_kernel,
        out_shape=jax.ShapeDtypeStruct((4, ROWS, LANES), F32),
        in_specs=[smem, smem, vmem],
        out_specs=vmem,
        scratch_shapes=scratch,
        compiler_params=pltpu.CompilerParams(
            collective_id=2, has_side_effects=True, vmem_limit_bytes=VMEM_LIMIT
        ),
    )(tile_slot, tile_list, grad)


def body(q_model, tile_slot, tile_list, rec_index, traces, adj_now, adj_prev, fwd_lap):
    tiles = gather_tiles(tile_slot, tile_list, q_model)
    grad, final = time_steps(rec_index, traces, adj_now, adj_prev, fwd_lap, tiles)
    return scatter_tiles(tile_slot, tile_list, grad), final


def solution(mesh):
    in_specs = (
        P("shot", "sub", None),
        P(),
        P(),
        P("shot", None),
        P("shot", None, None),
        P("shot", "sub", None),
        P("shot", "sub", None),
        P("shot", None, "sub", None),
    )
    out_specs = (P("shot", "sub", None), P("shot", "sub", None))
    return jax.shard_map(body, mesh=mesh, in_specs=in_specs, out_specs=out_specs, check_vma=False)
```

```python
import jax
import jax.numpy as jnp
import numpy as np
from jax import lax
from jax.experimental import pallas as pl
from jax.experimental.pallas import tpu as pltpu
from jax.sharding import PartitionSpec as P

TS = 16
STEPS = 8
ROWS = 32
LANES = 256
PLANE = 4096
COEFFS = (-205.0 / 72.0, 8.0 / 5.0, -1.0 / 5.0, 8.0 / 315.0, -1.0 / 560.0)
C1 = COEFFS[1]
REL = tuple(c / C1 for c in COEFFS)

NCH = 4
R = ROWS // NCH
HC = 8
CB = 32 // HC

MESH = pl.DeviceIdType.MESH
VMEM_LIMIT = 60 * 1024 * 1024
F32 = jnp.float32
BF16 = jnp.bfloat16
DIRS = ((0, 1), (1, -1))


def lateral_matrices():
    out = np.zeros((3, LANES, LANES), np.float32)
    k = np.arange(LANES)[:, None]
    n = np.arange(LANES)[None, :]
    for d in (-1, 0, 1):
        dx = 4 * d + k // 64 - n // 64
        dy = k % 64 - n % 64
        for reach in range(1, 5):
            hit = ((dx == 0) & (np.abs(dy) == reach)) | ((dy == 0) & (np.abs(dx) == reach))
            out[d + 1][hit] = REL[reach]
    return np.concatenate([out, out]).reshape(6 * LANES, LANES)


def shot_at(y, x, z):
    return (y * 4 + x) * 4 + z


def ring(v):
    return (v + 8) % 4


class Links:
    def __init__(self):
        me = lax.axis_index("shot")
        self.at = {"y": me // 16, "x": (me // 4) % 4, "z": me % 4}
        self.shot = me
        self.sub = lax.axis_index("sub")

    def step(self, axis, delta):
        at = dict(self.at)
        at[axis] = ring(at[axis] + delta)
        return shot_at(at["y"], at["x"], at["z"])

    def copy(self, axis, delta, src, dst, sems, c, k):
        return pltpu.make_async_remote_copy(
            src_ref=src,
            dst_ref=dst,
            send_sem=sems[0].at[c, k],
            recv_sem=sems[1].at[c, k],
            device_id=(self.step(axis, delta), self.sub),
            device_id_type=MESH,
        )


def axes_of(c):
    return ("x", "y") if c % 2 == 0 else ("y", "x")


def slot_parts(slot, order):
    if order == 0:
        return slot // 64, slot % 64
    return (slot // 16) % 4, (slot // 64) * 16 + slot % 16


class Gather:
    def __init__(self, links, ts, tl, q_ref, QF, g, rel_s, rel_r, blk_s, blk_r, sems):
        self.links, self.ts, self.tl, self.q_ref, self.QF = links, ts, tl, q_ref, QF
        self.g, self.rel_s, self.rel_r, self.blk_s, self.blk_r = g, rel_s, rel_r, blk_s, blk_r
        self.sems = sems
        self.sent = []
        self.live = {}

    def go(self, name, c, d, axis, delta, src, dst, k):
        copy = self.links.copy(axis, delta, src, dst, self.sems, c, k + d)
        copy.start()
        self.sent.append(copy)
        self.live[name, c, d] = copy

    def got(self, name, c, d):
        self.live[name, c, d].wait_recv()

    def line(self, c):
        return self.links.at[axes_of(c)[0]]

    def part(self, c, line, zz, t0=0, n=4):
        return self.g[c].at[pl.ds(line * 16 + zz * 4 + t0, n)]

    def start(self, c):
        z, line = self.links.at["z"], self.line(c)
        src = self.q_ref.at[:, pl.ds(c * R, R)]
        for d, delta in DIRS:
            self.go("zp1", c, d, "z", delta, src, self.part(c, line, z), 0)
        for d, delta in DIRS:
            self.go("a1own", c, d, axes_of(c)[0], delta, src, self.part(c, line, z), 4)

    def keep(self, c):
        z, line = self.links.at["z"], self.line(c)
        for t in range(4):
            self.g[c][line * 16 + z * 4 + t] = self.q_ref[t, c * R : (c + 1) * R, :]

    def zp2(self, c):
        z, line = self.links.at["z"], self.line(c)
        for d, delta in DIRS:
            self.got("zp1", c, d)
            piece = self.part(c, line, ring(z - delta), 2 * d, 2)
            self.go("zp2", c, d, "z", delta, piece, piece, 2)

    def spread(self, name, c, zz, k):
        piece = self.part(c, self.line(c), zz)
        for d, delta in DIRS:
            self.go(name, c, d, axes_of(c)[0], delta, piece, piece, k)

    def a1n(self, c):
        z = self.links.at["z"]
        self.spread("a1m", c, ring(z - 1), 6)
        self.spread("a1p", c, ring(z + 1), 8)

    def a1f(self, c):
        for d in range(2):
            self.got("zp2", c, d)
        self.spread("a1f", c, ring(self.links.at["z"] + 2), 10)

    def forward(self, come, name, c, zz, k):
        for d, delta in DIRS:
            self.got(come, c, d)
            piece = self.part(c, ring(self.line(c) - delta), zz, 2 * d, 2)
            self.go(name, c, d, axes_of(c)[0], delta, piece, piece, k)

    def a2own(self, c):
        self.forward("a1own", "a2own", c, self.links.at["z"], 12)

    def a2n(self, c):
        z = self.links.at["z"]
        self.forward("a1m", "a2m", c, ring(z - 1), 14)
        self.forward("a1p", "a2p", c, ring(z + 1), 16)

    def a2f(self, c):
        self.forward("a1f", "a2f", c, ring(self.links.at["z"] + 2), 18)

    def target(self, c, delta, p):
        slot = self.ts[self.tl[self.links.step(axes_of(c)[1], delta), p]]
        return slot_parts(slot, c % 2)

    def rel(self, c):
        last = axes_of(c)[1]
        for d in range(2):
            for name in ("a2own", "a2m", "a2p", "a2f"):
                self.got(name, c, d)
        for d, delta in DIRS:
            for p in range(8):
                _, at = self.target(c, 2, 8 * d + p)
                self.rel_s[c][d, p] = self.g[c][at]
            self.go("rel", c, d, last, delta, self.rel_s[c].at[d], self.rel_r[c].at[d], 20)

    def blk(self, c):
        last = axes_of(c)[1]
        mine = self.links.at[last]
        for d, delta in DIRS:
            self.got("rel", c, d)
            for p in range(16):
                owner, at = self.target(c, delta, p)
                value = self.g[c][at]
                if p // 8 == d:
                    value = jnp.where(owner == mine, value, self.rel_r[c][d, p % 8])
                self.blk_s[c][d, p] = value
            self.go("blk", c, d, last, delta, self.blk_s[c].at[d], self.blk_r[c].at[d], 22)

    def finish(self, c):
        mine = self.links.at[axes_of(c)[1]]
        blk_r = self.blk_r[c]
        for d in range(2):
            self.got("blk", c, d)
        for p in range(16):
            owner, at = self.target(c, 0, p)
            gap = ring(owner - mine)
            if p < 8:
                other = jnp.where(gap == 1, blk_r[1, p], blk_r[0, p])
            else:
                other = jnp.where(gap == 3, blk_r[0, p], blk_r[1, p])
            value = C1 * jnp.where(gap == 0, self.g[c][at], other)
            a, b = p // 4, p % 4
            for h in range(2):
                row = 32 * (2 * a + h) + c * R
                self.QF[row : row + R, 128 * b : 128 * b + 128] = value[:, 128 * h : 128 * h + 128]

    def drain(self):
        for copy in self.sent:
            copy.wait_send()


class Scatter:
    def __init__(
        self, links, tab, out_ref, gg, rel_s, rel_r, blk_s, blk_r, col, zrel_r, zblk_s, zblk_r, sems
    ):
        self.links, self.tab, self.out_ref, self.gg, self.col = links, tab, out_ref, gg, col
        self.rel_s, self.rel_r, self.blk_s, self.blk_r = rel_s, rel_r, blk_s, blk_r
        self.zrel_r, self.zblk_s, self.zblk_r = zrel_r, zblk_s, zblk_r
        self.sems = sems
        self.sent = []
        self.live = {}

    go = Gather.go
    got = Gather.got
    line = Gather.line
    drain = Gather.drain

    def first(self, c):
        return self.links.at[axes_of(c)[1]]

    def a1(self, c, half):
        for d, delta in DIRS:
            side = d if half == 0 else 1 - d
            piece = self.gg[c].at[pl.ds(self.first(c) * 16 + 8 * side, 8)]
            self.go(("a1", half), c, d, axes_of(c)[1], delta, piece, piece, 2 * half)

    def a2(self, c):
        for d, delta in DIRS:
            self.got(("a1", 0), c, d)
            piece = self.gg[c].at[pl.ds(ring(self.first(c) - delta) * 16 + 8 * d, 8)]
            self.go("a2", c, d, axes_of(c)[1], delta, piece, piece, 4)

    def partial(self, c, line, e):
        total = None
        for src in range(4):
            term = self.gg[c][self.tab[(c % 2) * 4 + src, line * 16 + e]]
            total = term if total is None else total + term
        return total

    def rel(self, c):
        for d in range(2):
            self.got(("a1", 1), c, d)
            self.got("a2", c, d)
        for d, delta in DIRS:
            for e in range(8):
                self.rel_s[c][d, e] = self.partial(c, ring(self.line(c) + 2), 8 * d + e)
            self.go(
                "rel", c, d, axes_of(c)[0], delta, self.rel_s[c].at[d], self.rel_r[c].at[d], 6
            )

    def own(self, c):
        for e in range(16):
            self.col[c][e] = self.partial(c, self.line(c), e)

    def blk(self, c):
        for d, delta in DIRS:
            self.got("rel", c, d)
            for e in range(16):
                value = self.partial(c, ring(self.line(c) + delta), e)
                if e // 8 == d:
                    value = value + self.rel_r[c][d, e % 8]
                self.blk_s[c][d, e] = value
            self.go(
                "blk", c, d, axes_of(c)[0], delta, self.blk_s[c].at[d], self.blk_r[c].at[d], 8
            )

    def zrel(self, c):
        z = self.links.at["z"]
        for d in range(2):
            self.got("blk", c, d)
        for e in range(16):
            self.col[c][e] += self.blk_r[c][0, e] + self.blk_r[c][1, e]
        for d, delta in DIRS:
            piece = self.col[c].at[pl.ds(ring(z + 2) * 4 + 2 * d, 2)]
            self.go("zrel", c, d, "z", delta, piece, self.zrel_r[c].at[d], 10)

    def zblk(self, c):
        z = self.links.at["z"]
        for d, delta in DIRS:
            self.got("zrel", c, d)
            for t in range(4):
                value = self.col[c][ring(z + delta) * 4 + t]
                if t // 2 == d:
                    value = value + self.zrel_r[c][d, t % 2]
                self.zblk_s[c][d, t] = value
            self.go("zblk", c, d, "z", delta, self.zblk_s[c].at[d], self.zblk_r[c].at[d], 12)

    def finish(self, c):
        z = self.links.at["z"]
        for d in range(2):
            self.got("zblk", c, d)
        for t in range(4):
            self.out_ref[t, c * R : (c + 1) * R, :] = (
                self.col[c][z * 4 + t] + self.zblk_r[c][0, t] + self.zblk_r[c][1, t]
            )


def split2(v):
    hi = v.astype(BF16)
    return hi, (v - hi.astype(F32)).astype(BF16)


def split3(v):
    hi = v.astype(BF16)
    rest = v - hi.astype(F32)
    mid = rest.astype(BF16)
    return hi, mid, (rest - mid.astype(F32)).astype(BF16)


def dot(a, b, transposed=False):
    dims = (((1,), (1,)), ((), ())) if transposed else (((1,), (0,)), ((), ()))
    return lax.dot_general(a, b, dims, preferred_element_type=F32)


def kernel(ts, tl, q_ref, rec, tr, u_in, w_in, fwd, mats, grad_out, fin_out, *scratch):
    scratch = list(scratch)

    def take(n):
        out = scratch[:n]
        del scratch[:n]
        return out

    U, H, LO, ACC, Q, G, S, PM, QF, T3, FW, hs, hr, tabv, tab = take(15)
    g, rel_s, rel_r, blk_s, blk_r = (take(NCH) for _ in range(5))
    gg, grel_s, grel_r, gblk_s, gblk_r = (take(NCH) for _ in range(5))
    col, zrel_r, zblk_s, zblk_r = (take(NCH) for _ in range(4))
    ssem, rsem, qs, qr, gs, gr, lsem = take(7)

    links = Links()
    shot, sub = links.shot, links.sub
    has_up, has_dn = sub > 0, sub < 3
    sides = ((has_up, sub - 1), (has_dn, sub + 1))
    load = pltpu.make_async_copy(fwd.at[0], FW, lsem.at[0])
    load.start()

    sem = pltpu.get_barrier_semaphore()
    for axis in ("y", "x", "z"):
        for delta in (1, -1):
            pl.semaphore_signal(
                sem, inc=1, device_id=(links.step(axis, delta), sub), device_id_type=MESH
            )
    for has, other in sides:

        @pl.when(has)
        def _():
            pl.semaphore_signal(sem, inc=1, device_id=(shot, other), device_id_type=MESH)

    pl.semaphore_wait(sem, 6 + has_up.astype(jnp.int32) + has_dn.astype(jnp.int32))

    def halo(slot, side, c):
        return pltpu.make_async_remote_copy(
            src_ref=hs.at[slot, side, c],
            dst_ref=hr.at[slot, 1 - side, c],
            send_sem=ssem.at[slot, side, c],
            recv_sem=rsem.at[slot, 1 - side, c],
            device_id=(shot, sides[side][1]),
            device_id_type=MESH,
        )

    def halo_in(slot, side, c):
        return pltpu.make_async_remote_copy(
            src_ref=hs.at[slot, side, c],
            dst_ref=hr.at[slot, side, c],
            send_sem=ssem.at[slot, side, c],
            recv_sem=rsem.at[slot, side, c],
            device_id=(shot, sides[side][1]),
            device_id_type=MESH,
        )

    def init_fields():
        zeros8 = jnp.zeros((32, 8, 128), F32)
        for par in range(2):
            U[par, :, 0:8, :] = zeros8
            U[par, :, 40:48, :] = zeros8
        for buf in (H, LO):
            buf[0:32, :] = jnp.zeros((32, LANES), BF16)
            buf[544:576, :] = jnp.zeros((32, LANES), BF16)
        for c in range(HC):
            for k in range(CB):
                cb = CB * c + k
                value = u_in[0, :, cb * 128 : (cb + 1) * 128]
                U[0, cb, 8:40, :] = value
                hs[0, 0, c, k] = value[0:4]
                hs[0, 1, c, k] = value[28:32]
                U[1, cb, 8:40, :] = w_in[0, :, cb * 128 : (cb + 1) * 128]
            for side in range(2):

                @pl.when(sides[side][0])
                def _():
                    halo(0, side, c).start()

        for j in range(16):
            hi, lo = split2(u_in[0, :, j * LANES : (j + 1) * LANES])
            H[32 + 32 * j : 64 + 32 * j, :] = hi
            LO[32 + 32 * j : 64 + 32 * j, :] = lo
        G[...] = jnp.zeros(G.shape, F32)

    receivers = rec[...]
    column = receivers & (PLANE - 1)
    level = (receivers >> 12) - sub * ROWS

    def source_values():
        depth_at = lax.broadcasted_iota(jnp.int32, (ROWS, LANES), 0)
        at_depth = depth_at == level
        for t in range(STEPS):
            value = jnp.where(at_depth, tr[0, t : t + 1, :], 0.0)
            for s, v in enumerate(split3(value)):
                T3[s, 32 * t : 32 * t + 32, 0:LANES] = v

    def source_block(j, carry):
        cell = lax.broadcasted_iota(jnp.int32, (LANES, LANES), 0)
        onehot = (cell + j * LANES == column).astype(F32).astype(BF16)
        total = dot(T3[0, :, 0:LANES], onehot, True)
        total = total + dot(T3[1, :, 0:LANES], onehot, True)
        total = total + dot(T3[2, :, 0:LANES], onehot, True)
        for t in range(STEPS):
            S[t, j] = total[32 * t : 32 * t + 32]
        return carry

    def sources(first, last):
        lax.fori_loop(first, last, source_block, 0)

    def permutation():
        src = lax.broadcasted_iota(jnp.int32, (512, 512), 0)
        dst = lax.broadcasted_iota(jnp.int32, (512, 512), 1)
        moved = ((src >> 4) & 7) * 64 + (src >> 7) * 16 + (src & 15)
        PM[...] = (moved == dst).astype(F32).astype(BF16)

    def table():
        row_at = lax.broadcasted_iota(jnp.int32, (8, 128), 0)
        lane_at = lax.broadcasted_iota(jnp.int32, (8, 128), 1)

        def table_row(p, acc):
            for order in range(2):
                first = ("y", "x")[order]
                m = links.at[first]
                for src in range(4):
                    slot = ts[tl[links.step(first, src - m), p]]
                    owner, at = slot_parts(slot, order)
                    at = jnp.where(owner == m, at, -1)
                    hit = (row_at == order * 4 + src) & (lane_at == at)
                    acc = jnp.where(hit, src * 16 + p, acc)
            return acc

        tabv[...] = lax.fori_loop(0, 16, table_row, jnp.full((8, 128), 64, jnp.int32))
        for c in range(NCH):
            gg[c][64] = jnp.zeros((R, LANES), F32)

    gather = Gather(links, ts, tl, q_ref, QF, g, rel_s, rel_r, blk_s, blk_r, (qs, qr))
    A, B = (0, 1), (2, 3)

    def each(step, chunks):
        for c in chunks:
            step(c)

    each(gather.start, A)
    each(gather.start, B)
    init_fields()
    each(gather.keep, A + B)
    each(gather.zp2, A)
    each(gather.a1n, A)
    each(gather.a2own, A)
    source_values()
    sources(0, 4)
    each(gather.zp2, B)
    each(gather.a1f, A)
    each(gather.a1n, B)
    each(gather.a2n, A)
    each(gather.a2own, B)
    sources(4, 8)
    each(gather.a2f, A)
    each(gather.a1f, B)
    each(gather.a2n, B)
    sources(8, 12)
    each(gather.rel, A)
    each(gather.a2f, B)
    sources(12, 16)
    each(gather.blk, A)
    permutation()
    each(gather.rel, B)
    table()
    fill = pltpu.make_async_copy(tabv, tab, lsem.at[1])
    fill.start()
    each(gather.finish, A)
    each(gather.blk, B)
    fill.wait()
    load.wait()
    each(gather.finish, B)
    gather.drain()

    for k in range(8):
        for s, v in enumerate(split3(QF[32 * k : 32 * k + 32, :])):
            T3[s, 32 * k : 32 * k + 32, :] = v
    for n in range(2):
        perm = PM[:, LANES * n : LANES * n + LANES]
        total = dot(T3[0], perm) + dot(T3[1], perm) + dot(T3[2], perm)
        for k in range(8):
            Q[2 * k + n] = total[32 * k : 32 * k + 32]

    def one_step(t, carry):
        par = lax.rem(t, 2)
        nxt = 1 - par
        wide = jnp.concatenate(
            [buf[32 * d : 32 * d + 512, :] for buf in (H, LO) for d in range(3)], axis=1
        )
        ACC[...] = dot(wide, mats[...])
        for c in range(HC):
            for side in range(2):

                @pl.when(sides[side][0])
                def _():
                    halo(par, side, c).wait_send()
                    halo_in(par, side, c).wait_recv()
                    first = 4 if side == 0 else 40
                    for k in range(CB):
                        U[par, CB * c + k, first : first + 4, :] = hr[par, side, c, k]

            for jj in range(CB // 2):
                j = CB // 2 * c + jj
                half = []
                for h in range(2):
                    cb = 2 * j + h
                    here = U[par, cb, 8:40, :]
                    lanes = slice(128 * h, 128 * h + 128)
                    acc = (3.0 * REL[0]) * here + ACC[32 * j : 32 * j + 32, lanes]
                    for reach in range(1, 5):
                        beside = U[par, cb, 8 + reach : 40 + reach, :] + U[par, cb, 8 - reach : 40 - reach, :]
                        acc = acc + (beside if reach == 1 else REL[reach] * beside)
                    new = 2.0 * here - U[nxt, cb, 8:40, :] + Q[j, :, lanes] * acc + S[t, j, :, lanes]
                    U[nxt, cb, 8:40, :] = new
                    hs[nxt, 0, c, 2 * jj + h] = new[0:4]
                    hs[nxt, 1, c, 2 * jj + h] = new[28:32]
                    G[j, :, lanes] += FW[t, :, cb * 128 : cb * 128 + 128].astype(F32) * new
                    half.append(new)
                hi, lo = split2(jnp.concatenate(half, axis=1))
                H[32 + 32 * j : 64 + 32 * j, :] = hi
                LO[32 + 32 * j : 64 + 32 * j, :] = lo
            for side in range(2):

                @pl.when(sides[side][0] & (t < STEPS - 1))
                def _():
                    halo(nxt, side, c).start()

        return carry

    lax.fori_loop(0, STEPS, one_step, 0)

    scatter = Scatter(
        links, tab, grad_out, gg, grel_s, grel_r, gblk_s, gblk_r, col, zrel_r, zblk_s, zblk_r, (gs, gr)
    )
    for k in range(8):
        wide = jnp.concatenate([G[2 * k], G[2 * k + 1]], axis=1)
        for s, v in enumerate(split3(wide)):
            T3[s, 32 * k : 32 * k + 32, :] = v
    for n in range(2):
        perm = PM[LANES * n : LANES * n + LANES, :]
        total = dot(T3[0], perm, True) + dot(T3[1], perm, True) + dot(T3[2], perm, True)
        for k in range(8):
            a, h = k // 2, k % 2
            for b in range(2):
                for c in range(NCH):
                    at = scatter.first(c) * 16 + 4 * a + 2 * n + b
                    row = 32 * k + c * R
                    gg[c][at, :, 128 * h : 128 * h + 128] = total[
                        row : row + R, 128 * b : 128 * b + 128
                    ]
    for c in A:
        scatter.a1(c, 0)
        scatter.a1(c, 1)
    for c in B:
        scatter.a1(c, 0)
    for cb in range(32):
        fin_out[0, :, cb * 128 : (cb + 1) * 128] = U[STEPS % 2, cb, 8:40, :].astype(BF16)
    each(scatter.a2, A)
    for c in B:
        scatter.a1(c, 1)
    each(scatter.a2, B)
    each(scatter.rel, A)
    each(scatter.own, A)
    each(scatter.blk, A)
    each(scatter.rel, B)
    each(scatter.own, B)
    each(scatter.zrel, A)
    each(scatter.blk, B)
    each(scatter.zblk, A)
    each(scatter.finish, A)
    each(scatter.zrel, B)
    each(scatter.zblk, B)
    each(scatter.finish, B)
    scatter.drain()


def body(q_model, tile_slot, tile_list, rec_index, traces, adj_now, adj_prev, fwd_lap):
    smem = pl.BlockSpec(memory_space=pltpu.SMEM)
    vmem = pl.BlockSpec(memory_space=pltpu.VMEM)
    mats = jnp.asarray(lateral_matrices(), BF16)
    scratch = [
        pltpu.VMEM((2, 32, 48, 128), F32),
        pltpu.VMEM((576, LANES), BF16),
        pltpu.VMEM((576, LANES), BF16),
        pltpu.VMEM((512, LANES), F32),
        pltpu.VMEM((16, ROWS, LANES), F32),
        pltpu.VMEM((16, ROWS, LANES), F32),
        pltpu.VMEM((STEPS, 16, ROWS, LANES), F32),
        pltpu.VMEM((512, 512), BF16),
        pltpu.VMEM((256, 512), F32),
        pltpu.VMEM((3, 256, 512), BF16),
        pltpu.VMEM((STEPS, ROWS, PLANE), BF16),
        pltpu.VMEM((2, 2, HC, CB, 4, 128), F32),
        pltpu.VMEM((2, 2, HC, CB, 4, 128), F32),
        pltpu.VMEM((8, 128), jnp.int32),
        pltpu.SMEM((8, 128), jnp.int32),
    ]
    scratch += [pltpu.VMEM((64, R, LANES), F32)] * NCH
    scratch += [pltpu.VMEM((2, 8, R, LANES), F32)] * (2 * NCH)
    scratch += [pltpu.VMEM((2, 16, R, LANES), F32)] * (2 * NCH)
    scratch += [pltpu.VMEM((65, R, LANES), F32)] * NCH
    scratch += [pltpu.VMEM((2, 8, R, LANES), F32)] * (2 * NCH)
    scratch += [pltpu.VMEM((2, 16, R, LANES), F32)] * (2 * NCH)
    scratch += [pltpu.VMEM((16, R, LANES), F32)] * NCH
    scratch += [pltpu.VMEM((2, 2, R, LANES), F32)] * NCH
    scratch += [pltpu.VMEM((2, 4, R, LANES), F32)] * (2 * NCH)
    scratch += [pltpu.SemaphoreType.DMA((2, 2, HC))] * 2
    scratch += [pltpu.SemaphoreType.DMA((NCH, 24))] * 2
    scratch += [pltpu.SemaphoreType.DMA((NCH, 14))] * 2
    scratch += [pltpu.SemaphoreType.DMA((2,))]
    return pl.pallas_call(
        kernel,
        out_shape=(
            jax.ShapeDtypeStruct((4, ROWS, LANES), F32),
            jax.ShapeDtypeStruct((1, ROWS, PLANE), BF16),
        ),
        in_specs=[smem, smem] + [vmem] * 5 + [pl.BlockSpec(memory_space=pl.ANY), vmem],
        out_specs=(vmem, vmem),
        scratch_shapes=scratch,
        compiler_params=pltpu.CompilerParams(
            collective_id=0, has_side_effects=True, vmem_limit_bytes=VMEM_LIMIT
        ),
    )(tile_slot, tile_list, q_model, rec_index, traces, adj_now, adj_prev, fwd_lap, mats)


def solution(mesh):
    in_specs = (
        P("shot", "sub", None),
        P(),
        P(),
        P("shot", None),
        P("shot", None, None),
        P("shot", "sub", None),
        P("shot", "sub", None),
        P("shot", None, "sub", None),
    )
    out_specs = (P("shot", "sub", None), P("shot", "sub", None))
    return jax.shard_map(body, mesh=mesh, in_specs=in_specs, out_specs=out_specs, check_vma=False)
```

```python
import jax
import jax.numpy as jnp
import numpy as np
from jax import lax
from jax.experimental import pallas as pl
from jax.experimental.pallas import tpu as pltpu
from jax.sharding import PartitionSpec as P

TS = 16
STEPS = 8
ROWS = 32
LANES = 256
PLANE = 4096
COEFFS = (-205.0 / 72.0, 8.0 / 5.0, -1.0 / 5.0, 8.0 / 315.0, -1.0 / 560.0)
C1 = COEFFS[1]
REL = tuple(c / C1 for c in COEFFS)

NCH = 4
R = ROWS // NCH
HC = 8
CB = 32 // HC

MESH = pl.DeviceIdType.MESH
VMEM_LIMIT = 60 * 1024 * 1024
F32 = jnp.float32
BF16 = jnp.bfloat16
DIRS = ((0, 1), (1, -1))


def lateral_matrices():
    out = np.zeros((3, LANES, LANES), np.float32)
    k = np.arange(LANES)[:, None]
    n = np.arange(LANES)[None, :]
    for d in (-1, 0, 1):
        dx = 4 * d + k // 64 - n // 64
        dy = k % 64 - n % 64
        for reach in range(1, 5):
            hit = ((dx == 0) & (np.abs(dy) == reach)) | ((dy == 0) & (np.abs(dx) == reach))
            out[d + 1][hit] = REL[reach]
    return np.concatenate([out, out]).reshape(6 * LANES, LANES)


def shot_at(y, x, z):
    return (y * 4 + x) * 4 + z


def ring(v):
    return (v + 8) & 3


class Links:
    def __init__(self):
        me = lax.axis_index("shot")
        self.at = {"y": me >> 4, "x": (me >> 2) & 3, "z": me & 3}
        self.shot = me
        self.sub = lax.axis_index("sub")

    def step(self, axis, delta):
        at = dict(self.at)
        at[axis] = ring(at[axis] + delta)
        return shot_at(at["y"], at["x"], at["z"])

    def copy(self, axis, delta, src, dst, sems, c, k):
        return pltpu.make_async_remote_copy(
            src_ref=src,
            dst_ref=dst,
            send_sem=sems[0].at[c, k],
            recv_sem=sems[1].at[c, k],
            device_id=(self.step(axis, delta), self.sub),
            device_id_type=MESH,
        )


def axes_of(c):
    return ("x", "y") if c % 2 == 0 else ("y", "x")


def slot_parts(slot, order):
    if order == 0:
        return slot >> 6, slot & 63
    return (slot >> 4) & 3, ((slot >> 6) << 4) + (slot & 15)


class Gather:
    def __init__(self, links, ts, tl, q_ref, QF, g, rel_s, rel_r, blk_s, blk_r, own_sem, sems):
        self.links, self.ts, self.tl, self.q_ref, self.QF = links, ts, tl, q_ref, QF
        self.g, self.rel_s, self.rel_r, self.blk_s, self.blk_r = g, rel_s, rel_r, blk_s, blk_r
        self.own_sem = own_sem
        self.kept = {}
        self.sems = sems
        self.sent = []
        self.live = {}

    def go(self, name, c, d, axis, delta, src, dst, k):
        copy = self.links.copy(axis, delta, src, dst, self.sems, c, k + d)
        copy.start()
        self.sent.append(copy)
        self.live[name, c, d] = copy

    def got(self, name, c, d):
        self.live[name, c, d].wait_recv()

    def line(self, c):
        return self.links.at[axes_of(c)[0]]

    def part(self, c, line, zz, t0=0, n=4):
        return self.g[c].at[pl.ds(line * 16 + zz * 4 + t0, n)]

    def start(self, c):
        z, line = self.links.at["z"], self.line(c)
        src = self.q_ref.at[:, pl.ds(c * R, R)]
        for d, delta in DIRS:
            self.go("zp1", c, d, "z", delta, src, self.part(c, line, z), 0)

    def own(self, c):
        z, line = self.links.at["z"], self.line(c)
        src = self.q_ref.at[:, pl.ds(c * R, R)]
        for d, delta in DIRS:
            self.go("a1own", c, d, axes_of(c)[0], delta, src, self.part(c, line, z), 4)

    def keep(self, c):
        z, line = self.links.at["z"], self.line(c)
        copy = pltpu.make_async_copy(
            self.q_ref.at[:, pl.ds(c * R, R)], self.part(c, line, z), self.own_sem.at[c]
        )
        copy.start()
        self.kept[c] = copy

    def zp2(self, c):
        z, line = self.links.at["z"], self.line(c)
        for d, delta in DIRS:
            self.got("zp1", c, d)
            piece = self.part(c, line, ring(z - delta), 2 * d, 2)
            self.go("zp2", c, d, "z", delta, piece, piece, 2)

    def spread(self, name, c, zz, k):
        piece = self.part(c, self.line(c), zz)
        for d, delta in DIRS:
            self.go(name, c, d, axes_of(c)[0], delta, piece, piece, k)

    def a1n(self, c):
        z = self.links.at["z"]
        self.spread("a1m", c, ring(z - 1), 6)
        self.spread("a1p", c, ring(z + 1), 8)

    def a1f(self, c):
        for d in range(2):
            self.got("zp2", c, d)
        self.spread("a1f", c, ring(self.links.at["z"] + 2), 10)

    def forward(self, come, name, c, zz, k):
        for d, delta in DIRS:
            self.got(come, c, d)
            piece = self.part(c, ring(self.line(c) - delta), zz, 2 * d, 2)
            self.go(name, c, d, axes_of(c)[0], delta, piece, piece, k)

    def a2own(self, c):
        self.forward("a1own", "a2own", c, self.links.at["z"], 12)

    def a2n(self, c):
        z = self.links.at["z"]
        self.forward("a1m", "a2m", c, ring(z - 1), 14)
        self.forward("a1p", "a2p", c, ring(z + 1), 16)

    def a2f(self, c):
        self.forward("a1f", "a2f", c, ring(self.links.at["z"] + 2), 18)

    def target(self, c, delta, p):
        slot = self.ts[self.tl[p, self.links.step(axes_of(c)[1], delta)]]
        return slot_parts(slot, c % 2)

    def rel(self, c):
        last = axes_of(c)[1]
        self.kept[c].wait()
        for d in range(2):
            for name in ("a2own", "a2m", "a2p", "a2f"):
                self.got(name, c, d)
        for d, delta in DIRS:
            for p in range(8):
                _, at = self.target(c, 2, 8 * d + p)
                self.rel_s[c][d, p] = self.g[c][at]
            self.go("rel", c, d, last, delta, self.rel_s[c].at[d], self.rel_r[c].at[d], 20)

    def half(self, name, c, d, delta, side, k):
        piece = pl.ds(8 * side, 8)
        self.go(
            name, c, d, axes_of(c)[1], delta,
            self.blk_s[c].at[d, piece], self.blk_r[c].at[d, piece], k,
        )

    def near(self, c):
        for d, delta in DIRS:
            for p in range(8 * (1 - d), 8 * (2 - d)):
                _, at = self.target(c, delta, p)
                self.blk_s[c][d, p] = self.g[c][at]
            self.half("near", c, d, delta, 1 - d, 24)

    def blk(self, c):
        mine = self.links.at[axes_of(c)[1]]
        for d, delta in DIRS:
            self.got("rel", c, d)
            for p in range(8 * d, 8 * (1 + d)):
                owner, at = self.target(c, delta, p)
                self.blk_s[c][d, p] = jnp.where(
                    owner == mine, self.g[c][at], self.rel_r[c][d, p % 8]
                )
            self.half("blk", c, d, delta, d, 22)

    def finish(self, c):
        mine = self.links.at[axes_of(c)[1]]
        blk_r = self.blk_r[c]
        for d in range(2):
            self.got("near", c, d)
            self.got("blk", c, d)
        for p in range(16):
            owner, at = self.target(c, 0, p)
            gap = ring(owner - mine)
            if p < 8:
                other = jnp.where(gap == 1, blk_r[1, p], blk_r[0, p])
            else:
                other = jnp.where(gap == 3, blk_r[0, p], blk_r[1, p])
            value = C1 * jnp.where(gap == 0, self.g[c][at], other)
            a, b = p // 4, p % 4
            for h in range(2):
                row = 32 * (2 * a + h) + c * R
                self.QF[row : row + R, 128 * b : 128 * b + 128] = value[:, 128 * h : 128 * h + 128]

    def drain(self):
        for copy in self.sent:
            copy.wait_send()


class Scatter:
    def __init__(
        self, links, tab, out_ref, GO, out_sem, gg, rel_s, rel_r, blk_s, blk_r, col, zrel_r, zblk_s, zblk_r, sems
    ):
        self.links, self.tab, self.out_ref, self.gg, self.col = links, tab, out_ref, gg, col
        self.rel_s, self.rel_r, self.blk_s, self.blk_r = rel_s, rel_r, blk_s, blk_r
        self.zrel_r, self.zblk_s, self.zblk_r = zrel_r, zblk_s, zblk_r
        self.GO, self.out_sem, self.outs = GO, out_sem, []
        self.sems = sems
        self.sent = []
        self.live = {}

    go = Gather.go
    got = Gather.got
    line = Gather.line
    drain = Gather.drain

    def first(self, c):
        return self.links.at[axes_of(c)[1]]

    def a1(self, c, half):
        for d, delta in DIRS:
            side = d if half == 0 else 1 - d
            piece = self.gg[c].at[pl.ds(self.first(c) * 16 + 8 * side, 8)]
            self.go(("a1", half), c, d, axes_of(c)[1], delta, piece, piece, 2 * half)

    def a2(self, c):
        for d, delta in DIRS:
            self.got(("a1", 0), c, d)
            piece = self.gg[c].at[pl.ds(ring(self.first(c) - delta) * 16 + 8 * d, 8)]
            self.go("a2", c, d, axes_of(c)[1], delta, piece, piece, 4)

    def partial(self, c, line, e):
        total = None
        for src in range(4):
            term = self.gg[c][self.tab[(c % 2) * 4 + src, line * 16 + e]]
            total = term if total is None else total + term
        return total

    def rel(self, c):
        for d in range(2):
            self.got(("a1", 1), c, d)
            self.got("a2", c, d)
        for d, delta in DIRS:
            for e in range(8):
                self.rel_s[c][d, e] = self.partial(c, ring(self.line(c) + 2), 8 * d + e)
            self.go(
                "rel", c, d, axes_of(c)[0], delta, self.rel_s[c].at[d], self.rel_r[c].at[d], 6
            )

    def own(self, c):
        for e in range(16):
            self.col[c][e] = self.partial(c, self.line(c), e)

    def half(self, name, c, d, delta, side, k):
        piece = pl.ds(8 * side, 8)
        self.go(
            name, c, d, axes_of(c)[0], delta,
            self.blk_s[c].at[d, piece], self.blk_r[c].at[d, piece], k,
        )

    def near(self, c):
        for d, delta in DIRS:
            for e in range(8 * (1 - d), 8 * (2 - d)):
                self.blk_s[c][d, e] = self.partial(c, ring(self.line(c) + delta), e)
            self.half("near", c, d, delta, 1 - d, 14)

    def blk(self, c):
        for d, delta in DIRS:
            self.got("rel", c, d)
            for e in range(8 * d, 8 * (1 + d)):
                value = self.partial(c, ring(self.line(c) + delta), e)
                self.blk_s[c][d, e] = value + self.rel_r[c][d, e % 8]
            self.half("blk", c, d, delta, d, 8)

    def zrel(self, c):
        z = self.links.at["z"]
        for d in range(2):
            self.got("near", c, d)
            self.got("blk", c, d)
        for e in range(16):
            self.col[c][e] += self.blk_r[c][0, e] + self.blk_r[c][1, e]
        for d, delta in DIRS:
            piece = self.col[c].at[pl.ds(ring(z + 2) * 4 + 2 * d, 2)]
            self.go("zrel", c, d, "z", delta, piece, self.zrel_r[c].at[d], 10)

    def znear(self, c):
        z = self.links.at["z"]
        for d, delta in DIRS:
            piece = self.col[c].at[pl.ds(ring(z + delta) * 4 + 2 * (1 - d), 2)]
            home = self.zblk_r[c].at[d, pl.ds(2 * (1 - d), 2)]
            self.go("znear", c, d, "z", delta, piece, home, 16)

    def zblk(self, c):
        z = self.links.at["z"]
        for d, delta in DIRS:
            self.got("zrel", c, d)
            for t in range(2):
                value = self.col[c][ring(z + delta) * 4 + 2 * d + t]
                self.zblk_s[c][d, t] = value + self.zrel_r[c][d, t]
            home = self.zblk_r[c].at[d, pl.ds(2 * d, 2)]
            self.go("zblk", c, d, "z", delta, self.zblk_s[c].at[d], home, 12)

    def finish(self, c):
        z = self.links.at["z"]
        for d in range(2):
            self.got("znear", c, d)
            self.got("zblk", c, d)
        for t in range(4):
            self.GO[c][t] = self.col[c][z * 4 + t] + self.zblk_r[c][0, t] + self.zblk_r[c][1, t]
        copy = pltpu.make_async_copy(
            self.GO[c], self.out_ref.at[:, pl.ds(c * R, R)], self.out_sem.at[c]
        )
        copy.start()
        self.outs.append(copy)


def split2(v):
    hi = v.astype(BF16)
    return hi, (v - hi.astype(F32)).astype(BF16)


def split3(v):
    hi = v.astype(BF16)
    rest = v - hi.astype(F32)
    mid = rest.astype(BF16)
    return hi, mid, (rest - mid.astype(F32)).astype(BF16)


def dot(a, b, transposed=False):
    dims = (((1,), (1,)), ((), ())) if transposed else (((1,), (0,)), ((), ()))
    return lax.dot_general(a, b, dims, preferred_element_type=F32)


def kernel(ts, tl, q_ref, rec, tr, u_hbm, w_hbm, fwd, mats_hbm, grad_out, fin_out, *scratch):
    scratch = list(scratch)

    def take(n):
        out = scratch[:n]
        del scratch[:n]
        return out

    U, H, LO, ACC, Q, G, S, PM, QF, T3, FW, hs, hr, tabv, tab, u_in, w_in, mats, FO = take(19)
    g, rel_s, rel_r, blk_s, blk_r = (take(NCH) for _ in range(5))
    gg, grel_s, grel_r, gblk_s, gblk_r = (take(NCH) for _ in range(5))
    col, zrel_r, zblk_s, zblk_r, GO = (take(NCH) for _ in range(5))
    ssem, rsem, qs, qr, gs, gr, lsem, own_sem, out_sem = take(9)

    links = Links()
    shot, sub = links.shot, links.sub
    has_up, has_dn = sub > 0, sub < 3
    sides = ((has_up, sub - 1), (has_dn, sub + 1))
    loads = [
        pltpu.make_async_copy(src, dst, lsem.at[k])
        for k, (src, dst) in enumerate(
            ((u_hbm, u_in), (w_hbm, w_in), (mats_hbm, mats), (fwd.at[0], FW))
        )
    ]

    sem = pltpu.get_barrier_semaphore()
    for axis in ("y", "x", "z"):
        for delta in (1, -1):
            pl.semaphore_signal(
                sem, inc=1, device_id=(links.step(axis, delta), sub), device_id_type=MESH
            )
    for has, other in sides:

        @pl.when(has)
        def _():
            pl.semaphore_signal(sem, inc=1, device_id=(shot, other), device_id_type=MESH)

    pl.semaphore_wait(sem, 6 + has_up.astype(jnp.int32) + has_dn.astype(jnp.int32))

    def halo(slot, side, c):
        return pltpu.make_async_remote_copy(
            src_ref=hs.at[slot, side, c],
            dst_ref=hr.at[slot, 1 - side, c],
            send_sem=ssem.at[slot, side, c],
            recv_sem=rsem.at[slot, 1 - side, c],
            device_id=(shot, sides[side][1]),
            device_id_type=MESH,
        )

    def halo_in(slot, side, c):
        return pltpu.make_async_remote_copy(
            src_ref=hs.at[slot, side, c],
            dst_ref=hr.at[slot, side, c],
            send_sem=ssem.at[slot, side, c],
            recv_sem=rsem.at[slot, side, c],
            device_id=(shot, sides[side][1]),
            device_id_type=MESH,
        )

    def init_fields():
        zeros8 = jnp.zeros((32, 8, 128), F32)
        for par in range(2):
            U[par, :, 0:8, :] = zeros8
            U[par, :, 40:48, :] = zeros8
        for buf in (H, LO):
            buf[0:32, :] = jnp.zeros((32, LANES), BF16)
            buf[544:576, :] = jnp.zeros((32, LANES), BF16)
        for c in range(HC):
            for k in range(CB):
                cb = CB * c + k
                value = u_in[0, :, cb * 128 : (cb + 1) * 128]
                U[0, cb, 8:40, :] = value
                hs[0, 0, c, k] = value[0:4]
                hs[0, 1, c, k] = value[28:32]
                U[1, cb, 8:40, :] = w_in[0, :, cb * 128 : (cb + 1) * 128]
            for side in range(2):

                @pl.when(sides[side][0])
                def _():
                    halo(0, side, c).start()

        for j in range(16):
            hi, lo = split2(u_in[0, :, j * LANES : (j + 1) * LANES])
            H[32 + 32 * j : 64 + 32 * j, :] = hi
            LO[32 + 32 * j : 64 + 32 * j, :] = lo
        G[...] = jnp.zeros(G.shape, F32)
        tabv[...] = jnp.full((8, 128), 64, jnp.int32)
        for c in range(NCH):
            gg[c][64] = jnp.zeros((R, LANES), F32)

    receivers = rec[...]
    column = receivers & (PLANE - 1)
    level = (receivers >> 12) - sub * ROWS

    def source_values():
        depth_at = lax.broadcasted_iota(jnp.int32, (ROWS, LANES), 0)
        at_depth = depth_at == level
        for t in range(STEPS):
            value = jnp.where(at_depth, tr[0, t : t + 1, :], 0.0)
            for s, v in enumerate(split3(value)):
                T3[s, 32 * t : 32 * t + 32, 0:LANES] = v

    def source_block(j, carry):
        cell = lax.broadcasted_iota(jnp.int32, (LANES, LANES), 0)
        onehot = (cell + j * LANES == column).astype(F32).astype(BF16)
        total = dot(T3[0, :, 0:LANES], onehot, True)
        total = total + dot(T3[1, :, 0:LANES], onehot, True)
        total = total + dot(T3[2, :, 0:LANES], onehot, True)
        for t in range(STEPS):
            S[t, j] = total[32 * t : 32 * t + 32]
        return carry

    def sources(first, last):
        lax.fori_loop(first, last, source_block, 0)

    def permutation():
        src = lax.broadcasted_iota(jnp.int32, (512, 512), 0)
        dst = lax.broadcasted_iota(jnp.int32, (512, 512), 1)
        moved = ((src >> 4) & 7) * 64 + (src >> 7) * 16 + (src & 15)
        PM[...] = (moved == dst).astype(F32).astype(BF16)

    def table_rows(acc, p):
        row_at = lax.broadcasted_iota(jnp.int32, (8, 128), 0)
        lane_at = lax.broadcasted_iota(jnp.int32, (8, 128), 1)
        for order in range(2):
            first = ("y", "x")[order]
            m = links.at[first]
            for src in range(4):
                slot = ts[tl[p, links.step(first, src - m)]]
                owner, at = slot_parts(slot, order)
                at = jnp.where(owner == m, at, -1)
                hit = (row_at == order * 4 + src) & (lane_at == at)
                acc = jnp.where(hit, src * 16 + p, acc)
        return acc

    gather = Gather(links, ts, tl, q_ref, QF, g, rel_s, rel_r, blk_s, blk_r, own_sem, (qs, qr))
    every = range(NCH)
    gather.start(0)
    gather.start(1)
    for copy in loads:
        copy.start()
    gather.own(0)
    gather.own(1)
    gather.start(2)
    gather.own(2)
    gather.start(3)
    gather.own(3)
    for c in every:
        gather.keep(c)
    source_values()
    sources(0, 4)
    permutation()
    gather.zp2(0)
    gather.a2own(0)
    gather.a2own(1)
    gather.zp2(1)
    gather.a1n(1)
    gather.a1n(0)
    sources(4, 8)
    gather.zp2(2)
    loads[0].wait()
    loads[1].wait()
    init_fields()
    gather.a1n(2)
    gather.zp2(3)
    gather.a1n(3)
    sources(8, 12)
    gather.a1f(0)
    gather.a1f(1)
    gather.a2n(1)
    gather.a1f(2)
    gather.a2n(0)
    gather.a1f(3)
    gather.a2f(0)
    gather.a2f(1)
    gather.a2n(3)
    gather.a2own(3)
    gather.a2own(2)
    sources(12, 16)
    gather.a2f(2)
    gather.a2n(2)
    gather.a2f(3)
    gather.rel(0)
    gather.rel(1)
    gather.near(1)
    gather.near(0)
    gather.rel(2)
    gather.rel(3)
    gather.near(2)
    gather.near(3)
    gather.blk(0)
    gather.blk(1)
    gather.blk(2)
    gather.blk(3)
    gather.finish(0)
    gather.finish(1)
    gather.finish(2)
    gather.finish(3)
    loads[2].wait()
    loads[3].wait()
    gather.drain()

    for k in range(8):
        for s, v in enumerate(split3(QF[32 * k : 32 * k + 32, :])):
            T3[s, 32 * k : 32 * k + 32, :] = v
    for n in range(2):
        perm = PM[:, LANES * n : LANES * n + LANES]
        total = dot(T3[0], perm) + dot(T3[1], perm) + dot(T3[2], perm)
        for k in range(8):
            Q[2 * k + n] = total[32 * k : 32 * k + 32]

    def one_step(t, carry):
        par = lax.rem(t, 2)
        nxt = 1 - par
        wide = jnp.concatenate(
            [buf[32 * d : 32 * d + 512, :] for buf in (H, LO) for d in range(3)], axis=1
        )
        ACC[...] = dot(wide, mats[...])
        tabv[...] = table_rows(table_rows(tabv[...], 2 * t), 2 * t + 1)
        for c in range(HC):
            for side in range(2):

                @pl.when(sides[side][0])
                def _():
                    halo(par, side, c).wait_send()
                    halo_in(par, side, c).wait_recv()
                    first = 4 if side == 0 else 40
                    for k in range(CB):
                        U[par, CB * c + k, first : first + 4, :] = hr[par, side, c, k]

            for jj in range(CB // 2):
                j = CB // 2 * c + jj
                half = []
                for h in range(2):
                    cb = 2 * j + h
                    here = U[par, cb, 8:40, :]
                    lanes = slice(128 * h, 128 * h + 128)
                    acc = (3.0 * REL[0]) * here + ACC[32 * j : 32 * j + 32, lanes]
                    for reach in range(1, 5):
                        beside = U[par, cb, 8 + reach : 40 + reach, :] + U[par, cb, 8 - reach : 40 - reach, :]
                        acc = acc + (beside if reach == 1 else REL[reach] * beside)
                    new = 2.0 * here - U[nxt, cb, 8:40, :] + Q[j, :, lanes] * acc + S[t, j, :, lanes]
                    U[nxt, cb, 8:40, :] = new
                    hs[nxt, 0, c, 2 * jj + h] = new[0:4]
                    hs[nxt, 1, c, 2 * jj + h] = new[28:32]
                    G[j, :, lanes] += FW[t, :, cb * 128 : cb * 128 + 128].astype(F32) * new
                    half.append(new)
                hi, lo = split2(jnp.concatenate(half, axis=1))
                H[32 + 32 * j : 64 + 32 * j, :] = hi
                LO[32 + 32 * j : 64 + 32 * j, :] = lo
            for side in range(2):

                @pl.when(sides[side][0] & (t < STEPS - 1))
                def _():
                    halo(nxt, side, c).start()

        return carry

    lax.fori_loop(0, STEPS, one_step, 0)
    fill = pltpu.make_async_copy(tabv, tab, lsem.at[4])
    fill.start()

    scatter = Scatter(
        links, tab, grad_out, GO, out_sem, gg, grel_s, grel_r, gblk_s, gblk_r, col, zrel_r, zblk_s, zblk_r, (gs, gr)
    )
    for k in range(8):
        wide = jnp.concatenate([G[2 * k], G[2 * k + 1]], axis=1)
        for s, v in enumerate(split3(wide)):
            T3[s, 32 * k : 32 * k + 32, :] = v
    for n in range(2):
        perm = PM[LANES * n : LANES * n + LANES, :]
        total = dot(T3[0], perm, True) + dot(T3[1], perm, True) + dot(T3[2], perm, True)
        for k in range(8):
            a, h = k // 2, k % 2
            for b in range(2):
                for c in range(NCH):
                    at = scatter.first(c) * 16 + 4 * a + 2 * n + b
                    row = 32 * k + c * R
                    gg[c][at, :, 128 * h : 128 * h + 128] = total[
                        row : row + R, 128 * b : 128 * b + 128
                    ]
    scatter.a1(3, 0)
    scatter.a1(1, 0)
    scatter.a1(3, 1)
    scatter.a1(2, 0)
    scatter.a1(0, 0)
    scatter.a1(2, 1)
    scatter.a1(1, 1)
    for cb in range(32):
        FO[0, :, cb * 128 : (cb + 1) * 128] = U[STEPS % 2, cb, 8:40, :].astype(BF16)
    final = pltpu.make_async_copy(FO, fin_out, out_sem.at[NCH])
    final.start()
    fill.wait()
    scatter.a2(3)
    scatter.a2(2)
    scatter.a2(0)
    scatter.a1(0, 1)
    scatter.a2(1)
    scatter.rel(2)
    scatter.rel(3)
    scatter.near(2)
    scatter.near(3)
    scatter.rel(0)
    scatter.rel(1)
    scatter.blk(2)
    scatter.own(3)
    scatter.blk(3)
    scatter.own(0)
    scatter.near(0)
    scatter.near(1)
    scatter.own(2)
    scatter.blk(0)
    scatter.own(1)
    scatter.zrel(2)
    scatter.blk(1)
    scatter.znear(2)
    scatter.zrel(3)
    scatter.znear(3)
    scatter.zrel(0)
    scatter.zblk(2)
    scatter.zrel(1)
    scatter.znear(1)
    scatter.znear(0)
    scatter.zblk(0)
    scatter.zblk(3)
    scatter.zblk(1)
    scatter.finish(0)
    scatter.finish(2)
    scatter.finish(3)
    scatter.finish(1)
    scatter.drain()
    final.wait()
    for copy in scatter.outs:
        copy.wait()


def hand_over(grad, final, grad_out, fin_out):
    grad_out[...] = grad[...]
    fin_out[...] = final[...]


def body(q_model, tile_slot, tile_list, rec_index, traces, adj_now, adj_prev, fwd_lap):
    smem = pl.BlockSpec(memory_space=pltpu.SMEM)
    vmem = pl.BlockSpec(memory_space=pltpu.VMEM)
    hbm = pl.BlockSpec(memory_space=pl.ANY)
    mats = jnp.asarray(lateral_matrices(), BF16)
    scratch = [
        pltpu.VMEM((2, 32, 48, 128), F32),
        pltpu.VMEM((576, LANES), BF16),
        pltpu.VMEM((576, LANES), BF16),
        pltpu.VMEM((512, LANES), F32),
        pltpu.VMEM((16, ROWS, LANES), F32),
        pltpu.VMEM((16, ROWS, LANES), F32),
        pltpu.VMEM((STEPS, 16, ROWS, LANES), F32),
        pltpu.VMEM((512, 512), BF16),
        pltpu.VMEM((256, 512), F32),
        pltpu.VMEM((3, 256, 512), BF16),
        pltpu.VMEM((STEPS, ROWS, PLANE), BF16),
        pltpu.VMEM((2, 2, HC, CB, 4, 128), F32),
        pltpu.VMEM((2, 2, HC, CB, 4, 128), F32),
        pltpu.VMEM((8, 128), jnp.int32),
        pltpu.SMEM((8, 128), jnp.int32),
        pltpu.VMEM((1, ROWS, PLANE), F32),
        pltpu.VMEM((1, ROWS, PLANE), F32),
        pltpu.VMEM((6 * LANES, LANES), BF16),
        pltpu.VMEM((1, ROWS, PLANE), BF16),
    ]
    scratch += [pltpu.VMEM((64, R, LANES), F32)] * NCH
    scratch += [pltpu.VMEM((2, 8, R, LANES), F32)] * (2 * NCH)
    scratch += [pltpu.VMEM((2, 16, R, LANES), F32)] * (2 * NCH)
    scratch += [pltpu.VMEM((65, R, LANES), F32)] * NCH
    scratch += [pltpu.VMEM((2, 8, R, LANES), F32)] * (2 * NCH)
    scratch += [pltpu.VMEM((2, 16, R, LANES), F32)] * (2 * NCH)
    scratch += [pltpu.VMEM((16, R, LANES), F32)] * NCH
    scratch += [pltpu.VMEM((2, 2, R, LANES), F32)] * NCH
    scratch += [pltpu.VMEM((2, 2, R, LANES), F32)] * NCH
    scratch += [pltpu.VMEM((2, 4, R, LANES), F32)] * NCH
    scratch += [pltpu.VMEM((4, R, LANES), F32)] * NCH
    scratch += [pltpu.SemaphoreType.DMA((2, 2, HC))] * 2
    scratch += [pltpu.SemaphoreType.DMA((NCH, 26))] * 2
    scratch += [pltpu.SemaphoreType.DMA((NCH, 18))] * 2
    scratch += [pltpu.SemaphoreType.DMA((5,)), pltpu.SemaphoreType.DMA((NCH,))]
    scratch += [pltpu.SemaphoreType.DMA((NCH + 1,))]
    grad, final = pl.pallas_call(
        kernel,
        out_shape=(
            jax.ShapeDtypeStruct((4, ROWS, LANES), F32),
            jax.ShapeDtypeStruct((1, ROWS, PLANE), BF16),
        ),
        in_specs=[smem, smem, hbm, vmem, vmem] + [hbm] * 4,
        out_specs=(hbm, hbm),
        scratch_shapes=scratch,
        compiler_params=pltpu.CompilerParams(
            collective_id=0, has_side_effects=True, vmem_limit_bytes=VMEM_LIMIT
        ),
    )(tile_slot, tile_list.T, q_model, rec_index, traces, adj_now, adj_prev, fwd_lap, mats)
    return pl.pallas_call(
        hand_over,
        out_shape=(
            jax.ShapeDtypeStruct(grad.shape, F32),
            jax.ShapeDtypeStruct(final.shape, BF16),
        ),
        in_specs=[vmem, vmem],
        out_specs=(vmem, vmem),
    )(grad, final)


def solution(mesh):
    in_specs = (
        P("shot", "sub", None),
        P(),
        P(),
        P("shot", None),
        P("shot", None, None),
        P("shot", "sub", None),
        P("shot", "sub", None),
        P("shot", None, "sub", None),
    )
    out_specs = (P("shot", "sub", None), P("shot", "sub", None))
    return jax.shard_map(body, mesh=mesh, in_specs=in_specs, out_specs=out_specs, check_vma=False)
```

```python
import jax
import jax.numpy as jnp
import numpy as np
from jax import lax
from jax.experimental import pallas as pl
from jax.experimental.pallas import tpu as pltpu
from jax.sharding import PartitionSpec as P

TS = 16
STEPS = 8
ROWS = 32
LANES = 256
PLANE = 4096
COEFFS = (-205.0 / 72.0, 8.0 / 5.0, -1.0 / 5.0, 8.0 / 315.0, -1.0 / 560.0)
C1 = COEFFS[1]
REL = tuple(c / C1 for c in COEFFS)

NCH = 4
R = ROWS // NCH
HC = 8
CB = 32 // HC

MESH = pl.DeviceIdType.MESH
VMEM_LIMIT = 60 * 1024 * 1024
F32 = jnp.float32
BF16 = jnp.bfloat16
DIRS = ((0, 1), (1, -1))


def lateral_matrices():
    out = np.zeros((3, LANES, LANES), np.float32)
    k = np.arange(LANES)[:, None]
    n = np.arange(LANES)[None, :]
    for d in (-1, 0, 1):
        dx = 4 * d + k // 64 - n // 64
        dy = k % 64 - n % 64
        for reach in range(1, 5):
            hit = ((dx == 0) & (np.abs(dy) == reach)) | ((dy == 0) & (np.abs(dx) == reach))
            out[d + 1][hit] = REL[reach]
    return np.concatenate([out, out]).reshape(6 * LANES, LANES)


def shot_at(y, x, z):
    return (y * 4 + x) * 4 + z


def ring(v):
    return (v + 8) & 3


class Links:
    def __init__(self):
        me = lax.axis_index("shot")
        self.at = {"y": me >> 4, "x": (me >> 2) & 3, "z": me & 3}
        self.shot = me
        self.sub = lax.axis_index("sub")

    def step(self, axis, delta):
        at = dict(self.at)
        at[axis] = ring(at[axis] + delta)
        return shot_at(at["y"], at["x"], at["z"])

    def copy(self, axis, delta, src, dst, sems, c, k):
        return pltpu.make_async_remote_copy(
            src_ref=src,
            dst_ref=dst,
            send_sem=sems[0].at[c, k],
            recv_sem=sems[1].at[c, k],
            device_id=(self.step(axis, delta), self.sub),
            device_id_type=MESH,
        )


def axes_of(c):
    return ("x", "y") if c % 2 == 0 else ("y", "x")


def slot_parts(slot, order):
    if order == 0:
        return slot >> 6, slot & 63
    return (slot >> 4) & 3, ((slot >> 6) << 4) + (slot & 15)


class Gather:
    def __init__(self, links, ts, tl, q_ref, QF, g, rel_s, rel_r, blk_s, blk_r, own_sem, sems):
        self.links, self.ts, self.tl, self.q_ref, self.QF = links, ts, tl, q_ref, QF
        self.g, self.rel_s, self.rel_r, self.blk_s, self.blk_r = g, rel_s, rel_r, blk_s, blk_r
        self.own_sem = own_sem
        self.kept = {}
        self.sems = sems
        self.sent = []
        self.live = {}

    def go(self, name, c, d, axis, delta, src, dst, k):
        copy = self.links.copy(axis, delta, src, dst, self.sems, c, k + d)
        copy.start()
        self.sent.append(copy)
        self.live[name, c, d] = copy

    def got(self, name, c, d):
        self.live[name, c, d].wait_recv()

    def line(self, c):
        return self.links.at[axes_of(c)[0]]

    def part(self, c, line, zz, t0=0, n=4):
        return self.g[c].at[pl.ds(line * 16 + zz * 4 + t0, n)]

    def start(self, c):
        self.kept[c].wait()
        piece = self.part(c, self.line(c), self.links.at["z"])
        for d, delta in DIRS:
            self.go("zp1", c, d, "z", delta, piece, piece, 0)

    def own(self, c):
        self.spread("a1own", c, self.links.at["z"], 4)

    def keep(self, c):
        z, line = self.links.at["z"], self.line(c)
        copy = pltpu.make_async_copy(
            self.q_ref.at[:, pl.ds(c * R, R)], self.part(c, line, z), self.own_sem.at[c]
        )
        copy.start()
        self.kept[c] = copy

    def zp2(self, c):
        z, line = self.links.at["z"], self.line(c)
        for d, delta in DIRS:
            self.got("zp1", c, d)
            piece = self.part(c, line, ring(z - delta), 2 * d, 2)
            self.go("zp2", c, d, "z", delta, piece, piece, 2)

    def spread(self, name, c, zz, k):
        piece = self.part(c, self.line(c), zz)
        for d, delta in DIRS:
            self.go(name, c, d, axes_of(c)[0], delta, piece, piece, k)

    def a1n(self, c):
        z = self.links.at["z"]
        self.spread("a1m", c, ring(z - 1), 6)
        self.spread("a1p", c, ring(z + 1), 8)

    def a1f(self, c):
        for d in range(2):
            self.got("zp2", c, d)
        self.spread("a1f", c, ring(self.links.at["z"] + 2), 10)

    def forward(self, come, name, c, zz, k):
        for d, delta in DIRS:
            self.got(come, c, d)
            piece = self.part(c, ring(self.line(c) - delta), zz, 2 * d, 2)
            self.go(name, c, d, axes_of(c)[0], delta, piece, piece, k)

    def a2own(self, c):
        self.forward("a1own", "a2own", c, self.links.at["z"], 12)

    def a2n(self, c):
        z = self.links.at["z"]
        self.forward("a1m", "a2m", c, ring(z - 1), 14)
        self.forward("a1p", "a2p", c, ring(z + 1), 16)

    def a2f(self, c):
        self.forward("a1f", "a2f", c, ring(self.links.at["z"] + 2), 18)

    def target(self, c, delta, p):
        slot = self.ts[self.tl[p, self.links.step(axes_of(c)[1], delta)]]
        return slot_parts(slot, c % 2)

    def rel(self, c):
        last = axes_of(c)[1]
        for d in range(2):
            for name in ("a2own", "a2m", "a2p", "a2f"):
                self.got(name, c, d)
        for d, delta in DIRS:
            for p in range(8):
                _, at = self.target(c, 2, 8 * d + p)
                self.rel_s[c][d, p] = self.g[c][at]
            self.go("rel", c, d, last, delta, self.rel_s[c].at[d], self.rel_r[c].at[d], 20)

    def half(self, name, c, d, delta, side, k):
        piece = pl.ds(8 * side, 8)
        self.go(
            name, c, d, axes_of(c)[1], delta,
            self.blk_s[c].at[d, piece], self.blk_r[c].at[d, piece], k,
        )

    def near(self, c):
        for d, delta in DIRS:
            for p in range(8 * (1 - d), 8 * (2 - d)):
                _, at = self.target(c, delta, p)
                self.blk_s[c][d, p] = self.g[c][at]
            self.half("near", c, d, delta, 1 - d, 24)

    def blk(self, c):
        mine = self.links.at[axes_of(c)[1]]
        for d, delta in DIRS:
            self.got("rel", c, d)
            for p in range(8 * d, 8 * (1 + d)):
                owner, at = self.target(c, delta, p)
                self.blk_s[c][d, p] = jnp.where(
                    owner == mine, self.g[c][at], self.rel_r[c][d, p % 8]
                )
            self.half("blk", c, d, delta, d, 22)

    def finish(self, c):
        mine = self.links.at[axes_of(c)[1]]
        blk_r = self.blk_r[c]
        for d in range(2):
            self.got("near", c, d)
            self.got("blk", c, d)
        for p in range(16):
            owner, at = self.target(c, 0, p)
            gap = ring(owner - mine)
            if p < 8:
                other = jnp.where(gap == 1, blk_r[1, p], blk_r[0, p])
            else:
                other = jnp.where(gap == 3, blk_r[0, p], blk_r[1, p])
            value = C1 * jnp.where(gap == 0, self.g[c][at], other)
            a, b = p // 4, p % 4
            for h in range(2):
                row = 32 * (2 * a + h) + c * R
                self.QF[row : row + R, 128 * b : 128 * b + 128] = value[:, 128 * h : 128 * h + 128]

    def drain(self):
        for copy in self.sent:
            copy.wait_send()


class Scatter:
    def __init__(
        self, links, tab, out_ref, GO, out_sem, gg, rel_s, rel_r, blk_s, blk_r, col, zrel_r, zblk_s, zblk_r, sems
    ):
        self.links, self.tab, self.out_ref, self.gg, self.col = links, tab, out_ref, gg, col
        self.rel_s, self.rel_r, self.blk_s, self.blk_r = rel_s, rel_r, blk_s, blk_r
        self.zrel_r, self.zblk_s, self.zblk_r = zrel_r, zblk_s, zblk_r
        self.GO, self.out_sem, self.outs = GO, out_sem, []
        self.sems = sems
        self.sent = []
        self.live = {}

    go = Gather.go
    got = Gather.got
    line = Gather.line
    drain = Gather.drain

    def first(self, c):
        return self.links.at[axes_of(c)[1]]

    def a1(self, c, half):
        for d, delta in DIRS:
            side = d if half == 0 else 1 - d
            piece = self.gg[c].at[pl.ds(self.first(c) * 16 + 8 * side, 8)]
            self.go(("a1", half), c, d, axes_of(c)[1], delta, piece, piece, 2 * half)

    def a2(self, c):
        for d, delta in DIRS:
            self.got(("a1", 0), c, d)
            piece = self.gg[c].at[pl.ds(ring(self.first(c) - delta) * 16 + 8 * d, 8)]
            self.go("a2", c, d, axes_of(c)[1], delta, piece, piece, 4)

    def partial(self, c, line, e):
        total = None
        for src in range(4):
            term = self.gg[c][self.tab[(c % 2) * 4 + src, line * 16 + e]]
            total = term if total is None else total + term
        return total

    def rel(self, c):
        for d in range(2):
            self.got(("a1", 1), c, d)
            self.got("a2", c, d)
        for d, delta in DIRS:
            for e in range(8):
                self.rel_s[c][d, e] = self.partial(c, ring(self.line(c) + 2), 8 * d + e)
            self.go(
                "rel", c, d, axes_of(c)[0], delta, self.rel_s[c].at[d], self.rel_r[c].at[d], 6
            )

    def own(self, c):
        for e in range(16):
            self.col[c][e] = self.partial(c, self.line(c), e)

    def half(self, name, c, d, delta, side, k):
        piece = pl.ds(8 * side, 8)
        self.go(
            name, c, d, axes_of(c)[0], delta,
            self.blk_s[c].at[d, piece], self.blk_r[c].at[d, piece], k,
        )

    def near(self, c):
        for d, delta in DIRS:
            for e in range(8 * (1 - d), 8 * (2 - d)):
                self.blk_s[c][d, e] = self.partial(c, ring(self.line(c) + delta), e)
            self.half("near", c, d, delta, 1 - d, 14)

    def blk(self, c):
        for d, delta in DIRS:
            self.got("rel", c, d)
            for e in range(8 * d, 8 * (1 + d)):
                value = self.partial(c, ring(self.line(c) + delta), e)
                self.blk_s[c][d, e] = value + self.rel_r[c][d, e % 8]
            self.half("blk", c, d, delta, d, 8)

    def zrel(self, c):
        z = self.links.at["z"]
        for d in range(2):
            self.got("near", c, d)
            self.got("blk", c, d)
        for e in range(16):
            self.col[c][e] += self.blk_r[c][0, e] + self.blk_r[c][1, e]
        for d, delta in DIRS:
            piece = self.col[c].at[pl.ds(ring(z + 2) * 4 + 2 * d, 2)]
            self.go("zrel", c, d, "z", delta, piece, self.zrel_r[c].at[d], 10)

    def znear(self, c):
        z = self.links.at["z"]
        for d, delta in DIRS:
            piece = self.col[c].at[pl.ds(ring(z + delta) * 4 + 2 * (1 - d), 2)]
            home = self.zblk_r[c].at[d, pl.ds(2 * (1 - d), 2)]
            self.go("znear", c, d, "z", delta, piece, home, 16)

    def zblk(self, c):
        z = self.links.at["z"]
        for d, delta in DIRS:
            self.got("zrel", c, d)
            for t in range(2):
                value = self.col[c][ring(z + delta) * 4 + 2 * d + t]
                self.zblk_s[c][d, t] = value + self.zrel_r[c][d, t]
            home = self.zblk_r[c].at[d, pl.ds(2 * d, 2)]
            self.go("zblk", c, d, "z", delta, self.zblk_s[c].at[d], home, 12)

    def finish(self, c):
        z = self.links.at["z"]
        for d in range(2):
            self.got("znear", c, d)
            self.got("zblk", c, d)
        for t in range(4):
            self.GO[c][t] = self.col[c][z * 4 + t] + self.zblk_r[c][0, t] + self.zblk_r[c][1, t]
        copy = pltpu.make_async_copy(
            self.GO[c], self.out_ref.at[:, pl.ds(c * R, R)], self.out_sem.at[c]
        )
        copy.start()
        self.outs.append(copy)


def split2(v):
    hi = v.astype(BF16)
    return hi, (v - hi.astype(F32)).astype(BF16)


def split3(v):
    hi = v.astype(BF16)
    rest = v - hi.astype(F32)
    mid = rest.astype(BF16)
    return hi, mid, (rest - mid.astype(F32)).astype(BF16)


def dot(a, b, transposed=False):
    dims = (((1,), (1,)), ((), ())) if transposed else (((1,), (0,)), ((), ()))
    return lax.dot_general(a, b, dims, preferred_element_type=F32)


def kernel(ts_hbm, tl_hbm, q_ref, rec_hbm, tr_hbm, u_hbm, w_hbm, fwd, mats_hbm, grad_out, fin_out, *scratch):
    scratch = list(scratch)

    def take(n):
        out = scratch[:n]
        del scratch[:n]
        return out

    U, H, LO, ACC, Q, G, S, PM, QF, T3, FW, hs, hr, tabv, tab, u_in, w_in, mats, FO, ts, tl, rec, tr = take(23)
    g, rel_s, rel_r, blk_s, blk_r = (take(NCH) for _ in range(5))
    gg, grel_s, grel_r, gblk_s, gblk_r = (take(NCH) for _ in range(5))
    col, zrel_r, zblk_s, zblk_r, GO = (take(NCH) for _ in range(5))
    ssem, rsem, qs, qr, gs, gr, lsem, own_sem, out_sem = take(9)

    links = Links()
    shot, sub = links.shot, links.sub
    has_up, has_dn = sub > 0, sub < 3
    sides = ((has_up, sub - 1), (has_dn, sub + 1))
    loads = [
        pltpu.make_async_copy(src, dst, lsem.at[k])
        for k, (src, dst) in enumerate(
            (
                (rec_hbm, rec), (tr_hbm, tr), (ts_hbm, ts), (tl_hbm, tl),
                (u_hbm, u_in), (w_hbm, w_in), (mats_hbm, mats), (fwd.at[0], FW),
            )
        )
    ]

    sem = pltpu.get_barrier_semaphore()
    for axis in ("y", "x", "z"):
        for delta in (1, -1):
            pl.semaphore_signal(
                sem, inc=1, device_id=(links.step(axis, delta), sub), device_id_type=MESH
            )
    for has, other in sides:

        @pl.when(has)
        def _():
            pl.semaphore_signal(sem, inc=1, device_id=(shot, other), device_id_type=MESH)

    gather = Gather(links, ts, tl, q_ref, QF, g, rel_s, rel_r, blk_s, blk_r, own_sem, (qs, qr))
    for c in range(NCH):
        gather.keep(c)
    for copy in loads:
        copy.start()

    def halo(slot, side, c):
        return pltpu.make_async_remote_copy(
            src_ref=hs.at[slot, side, c],
            dst_ref=hr.at[slot, 1 - side, c],
            send_sem=ssem.at[slot, side, c],
            recv_sem=rsem.at[slot, 1 - side, c],
            device_id=(shot, sides[side][1]),
            device_id_type=MESH,
        )

    def halo_in(slot, side, c):
        return pltpu.make_async_remote_copy(
            src_ref=hs.at[slot, side, c],
            dst_ref=hr.at[slot, side, c],
            send_sem=ssem.at[slot, side, c],
            recv_sem=rsem.at[slot, side, c],
            device_id=(shot, sides[side][1]),
            device_id_type=MESH,
        )

    def init_fields():
        zeros8 = jnp.zeros((32, 8, 128), F32)
        for par in range(2):
            U[par, :, 0:8, :] = zeros8
            U[par, :, 40:48, :] = zeros8
        for buf in (H, LO):
            buf[0:32, :] = jnp.zeros((32, LANES), BF16)
            buf[544:576, :] = jnp.zeros((32, LANES), BF16)
        for c in range(HC):
            for k in range(CB):
                cb = CB * c + k
                value = u_in[0, :, cb * 128 : (cb + 1) * 128]
                U[0, cb, 8:40, :] = value
                hs[0, 0, c, k] = value[0:4]
                hs[0, 1, c, k] = value[28:32]
                U[1, cb, 8:40, :] = w_in[0, :, cb * 128 : (cb + 1) * 128]
            for side in range(2):

                @pl.when(sides[side][0])
                def _():
                    halo(0, side, c).start()

        for j in range(16):
            hi, lo = split2(u_in[0, :, j * LANES : (j + 1) * LANES])
            H[32 + 32 * j : 64 + 32 * j, :] = hi
            LO[32 + 32 * j : 64 + 32 * j, :] = lo
        G[...] = jnp.zeros(G.shape, F32)
        tabv[...] = jnp.full((8, 128), 64, jnp.int32)
        for c in range(NCH):
            gg[c][64] = jnp.zeros((R, LANES), F32)

    loads[0].wait()
    loads[1].wait()
    receivers = rec[...]
    column = receivers & (PLANE - 1)
    level = (receivers >> 12) - sub * ROWS

    def source_values():
        depth_at = lax.broadcasted_iota(jnp.int32, (ROWS, LANES), 0)
        at_depth = depth_at == level
        for t in range(STEPS):
            value = jnp.where(at_depth, tr[0, t : t + 1, :], 0.0)
            for s, v in enumerate(split3(value)):
                T3[s, 32 * t : 32 * t + 32, 0:LANES] = v

    def source_block(j, carry):
        cell = lax.broadcasted_iota(jnp.int32, (LANES, LANES), 0)
        onehot = (cell + j * LANES == column).astype(F32).astype(BF16)
        total = dot(T3[0, :, 0:LANES], onehot, True)
        total = total + dot(T3[1, :, 0:LANES], onehot, True)
        total = total + dot(T3[2, :, 0:LANES], onehot, True)
        for t in range(STEPS):
            S[t, j] = total[32 * t : 32 * t + 32]
        return carry

    def sources(first, last):
        lax.fori_loop(first, last, source_block, 0)

    def permutation():
        src = lax.broadcasted_iota(jnp.int32, (512, 512), 0)
        dst = lax.broadcasted_iota(jnp.int32, (512, 512), 1)
        moved = ((src >> 4) & 7) * 64 + (src >> 7) * 16 + (src & 15)
        PM[...] = (moved == dst).astype(F32).astype(BF16)

    def lateral():
        wide = jnp.concatenate(
            [buf[32 * d : 32 * d + 512, :] for buf in (H, LO) for d in range(3)], axis=1
        )
        ACC[...] = dot(wide, mats[...])

    def table_rows(acc, p):
        row_at = lax.broadcasted_iota(jnp.int32, (8, 128), 0)
        lane_at = lax.broadcasted_iota(jnp.int32, (8, 128), 1)
        for order in range(2):
            first = ("y", "x")[order]
            m = links.at[first]
            for src in range(4):
                slot = ts[tl[p, links.step(first, src - m)]]
                owner, at = slot_parts(slot, order)
                at = jnp.where(owner == m, at, -1)
                hit = (row_at == order * 4 + src) & (lane_at == at)
                acc = jnp.where(hit, src * 16 + p, acc)
        return acc

    source_values()
    permutation()
    pl.semaphore_wait(sem, 6 + has_up.astype(jnp.int32) + has_dn.astype(jnp.int32))
    every = range(NCH)
    gather.start(0)
    gather.start(1)
    gather.own(0)
    gather.own(1)
    gather.start(2)
    gather.own(2)
    gather.start(3)
    gather.own(3)
    sources(0, 4)
    gather.zp2(0)
    gather.a2own(0)
    gather.a2own(1)
    gather.zp2(1)
    gather.a1n(1)
    gather.a1n(0)
    sources(4, 8)
    gather.zp2(2)
    loads[4].wait()
    loads[5].wait()
    init_fields()
    loads[6].wait()
    lateral()
    gather.a1n(2)
    gather.zp2(3)
    gather.a1n(3)
    sources(8, 12)
    gather.a1f(0)
    gather.a1f(1)
    gather.a2n(1)
    gather.a1f(2)
    gather.a2n(0)
    gather.a1f(3)
    gather.a2f(0)
    gather.a2f(1)
    gather.a2n(3)
    gather.a2own(3)
    gather.a2own(2)
    sources(12, 16)
    gather.a2f(2)
    gather.a2n(2)
    gather.a2f(3)
    loads[2].wait()
    loads[3].wait()
    gather.rel(0)
    gather.rel(1)
    gather.near(1)
    gather.near(0)
    gather.rel(2)
    gather.rel(3)
    gather.near(2)
    gather.near(3)
    gather.blk(0)
    gather.blk(1)
    gather.blk(2)
    gather.blk(3)
    gather.finish(0)
    gather.finish(1)
    gather.finish(2)
    gather.finish(3)
    loads[7].wait()
    gather.drain()

    for k in range(8):
        for s, v in enumerate(split2(QF[32 * k : 32 * k + 32, :])):
            T3[s, 32 * k : 32 * k + 32, :] = v
    for n in range(2):
        perm = PM[:, LANES * n : LANES * n + LANES]
        total = dot(T3[0], perm) + dot(T3[1], perm)
        for k in range(8):
            Q[2 * k + n] = total[32 * k : 32 * k + 32]

    def one_step(t, carry):
        par = lax.rem(t, 2)
        nxt = 1 - par
        for c in range(HC):
            for side in range(2):

                @pl.when(sides[side][0])
                def _():
                    halo(par, side, c).wait_send()
                    halo_in(par, side, c).wait_recv()
                    first = 4 if side == 0 else 40
                    for k in range(CB):
                        U[par, CB * c + k, first : first + 4, :] = hr[par, side, c, k]

            for jj in range(CB // 2):
                j = CB // 2 * c + jj
                half = []
                for h in range(2):
                    cb = 2 * j + h
                    here = U[par, cb, 8:40, :]
                    lanes = slice(128 * h, 128 * h + 128)
                    acc = (3.0 * REL[0]) * here + ACC[32 * j : 32 * j + 32, lanes]
                    for reach in range(1, 5):
                        beside = U[par, cb, 8 + reach : 40 + reach, :] + U[par, cb, 8 - reach : 40 - reach, :]
                        acc = acc + (beside if reach == 1 else REL[reach] * beside)
                    new = 2.0 * here - U[nxt, cb, 8:40, :] + Q[j, :, lanes] * acc + S[t, j, :, lanes]
                    U[nxt, cb, 8:40, :] = new
                    hs[nxt, 0, c, 2 * jj + h] = new[0:4]
                    hs[nxt, 1, c, 2 * jj + h] = new[28:32]
                    G[j, :, lanes] += FW[t, :, cb * 128 : cb * 128 + 128].astype(F32) * new
                    half.append(new)
                hi, lo = split2(jnp.concatenate(half, axis=1))
                H[32 + 32 * j : 64 + 32 * j, :] = hi
                LO[32 + 32 * j : 64 + 32 * j, :] = lo
            for side in range(2):

                @pl.when(sides[side][0] & (t < STEPS - 1))
                def _():
                    halo(nxt, side, c).start()

        pl.when(t < STEPS - 1)(lateral)
        tabv[...] = table_rows(table_rows(tabv[...], 2 * t), 2 * t + 1)
        return carry

    lax.fori_loop(0, STEPS, one_step, 0)
    fill = pltpu.make_async_copy(tabv, tab, lsem.at[8])
    fill.start()

    scatter = Scatter(
        links, tab, grad_out, GO, out_sem, gg, grel_s, grel_r, gblk_s, gblk_r, col, zrel_r, zblk_s, zblk_r, (gs, gr)
    )
    for k in range(8):
        wide = jnp.concatenate([G[2 * k], G[2 * k + 1]], axis=1)
        for s, v in enumerate(split2(wide)):
            T3[s, 32 * k : 32 * k + 32, :] = v
    for n in range(2):
        perm = PM[LANES * n : LANES * n + LANES, :]
        total = dot(T3[0], perm, True) + dot(T3[1], perm, True)
        for k in range(8):
            a, h = k // 2, k % 2
            for b in range(2):
                for c in range(NCH):
                    at = scatter.first(c) * 16 + 4 * a + 2 * n + b
                    row = 32 * k + c * R
                    gg[c][at, :, 128 * h : 128 * h + 128] = total[
                        row : row + R, 128 * b : 128 * b + 128
                    ]
    scatter.a1(1, 0)
    scatter.a1(0, 0)
    scatter.a1(2, 0)
    scatter.a1(3, 0)
    scatter.a1(3, 1)
    scatter.a1(0, 1)
    for cb in range(32):
        FO[0, :, cb * 128 : (cb + 1) * 128] = U[STEPS % 2, cb, 8:40, :].astype(BF16)
    final = pltpu.make_async_copy(FO, fin_out, out_sem.at[NCH])
    final.start()
    fill.wait()
    scatter.a2(0)
    scatter.a1(1, 1)
    scatter.a1(2, 1)
    scatter.a2(1)
    scatter.a2(3)
    scatter.a2(2)
    scatter.rel(0)
    scatter.rel(1)
    scatter.near(0)
    scatter.own(0)
    scatter.rel(3)
    scatter.rel(2)
    scatter.blk(0)
    scatter.near(1)
    scatter.near(2)
    scatter.blk(1)
    scatter.near(3)
    scatter.blk(3)
    scatter.blk(2)
    scatter.zrel(0)
    scatter.own(2)
    scatter.znear(0)
    scatter.own(1)
    scatter.own(3)
    scatter.zrel(1)
    scatter.znear(1)
    scatter.zrel(2)
    scatter.znear(2)
    scatter.zrel(3)
    scatter.zblk(0)
    scatter.zblk(1)
    scatter.znear(3)
    scatter.zblk(2)
    scatter.zblk(3)
    scatter.finish(2)
    scatter.finish(0)
    scatter.finish(1)
    scatter.finish(3)
    scatter.drain()
    final.wait()
    for copy in scatter.outs:
        copy.wait()


def hand_over(grad, final, grad_out, fin_out):
    grad_out[...] = grad[...]
    fin_out[...] = final[...]


def body(q_model, tile_slot, tile_list, rec_index, traces, adj_now, adj_prev, fwd_lap):
    vmem = pl.BlockSpec(memory_space=pltpu.VMEM)
    hbm = pl.BlockSpec(memory_space=pl.ANY)
    mats = jnp.asarray(lateral_matrices(), BF16)
    scratch = [
        pltpu.VMEM((2, 32, 48, 128), F32),
        pltpu.VMEM((576, LANES), BF16),
        pltpu.VMEM((576, LANES), BF16),
        pltpu.VMEM((512, LANES), F32),
        pltpu.VMEM((16, ROWS, LANES), F32),
        pltpu.VMEM((16, ROWS, LANES), F32),
        pltpu.VMEM((STEPS, 16, ROWS, LANES), F32),
        pltpu.VMEM((512, 512), BF16),
        pltpu.VMEM((256, 512), F32),
        pltpu.VMEM((3, 256, 512), BF16),
        pltpu.VMEM((STEPS, ROWS, PLANE), BF16),
        pltpu.VMEM((2, 2, HC, CB, 4, 128), F32),
        pltpu.VMEM((2, 2, HC, CB, 4, 128), F32),
        pltpu.VMEM((8, 128), jnp.int32),
        pltpu.SMEM((8, 128), jnp.int32),
        pltpu.VMEM((1, ROWS, PLANE), F32),
        pltpu.VMEM((1, ROWS, PLANE), F32),
        pltpu.VMEM((6 * LANES, LANES), BF16),
        pltpu.VMEM((1, ROWS, PLANE), BF16),
        pltpu.SMEM((256,), jnp.int32),
        pltpu.SMEM((16, 64), jnp.int32),
        pltpu.VMEM((1, LANES), jnp.int32),
        pltpu.VMEM((1, STEPS, LANES), F32),
    ]
    scratch += [pltpu.VMEM((64, R, LANES), F32)] * NCH
    scratch += [pltpu.VMEM((2, 8, R, LANES), F32)] * (2 * NCH)
    scratch += [pltpu.VMEM((2, 16, R, LANES), F32)] * (2 * NCH)
    scratch += [pltpu.VMEM((65, R, LANES), F32)] * NCH
    scratch += [pltpu.VMEM((2, 8, R, LANES), F32)] * (2 * NCH)
    scratch += [pltpu.VMEM((2, 16, R, LANES), F32)] * (2 * NCH)
    scratch += [pltpu.VMEM((16, R, LANES), F32)] * NCH
    scratch += [pltpu.VMEM((2, 2, R, LANES), F32)] * NCH
    scratch += [pltpu.VMEM((2, 2, R, LANES), F32)] * NCH
    scratch += [pltpu.VMEM((2, 4, R, LANES), F32)] * NCH
    scratch += [pltpu.VMEM((4, R, LANES), F32)] * NCH
    scratch += [pltpu.SemaphoreType.DMA((2, 2, HC))] * 2
    scratch += [pltpu.SemaphoreType.DMA((NCH, 26))] * 2
    scratch += [pltpu.SemaphoreType.DMA((NCH, 18))] * 2
    scratch += [pltpu.SemaphoreType.DMA((9,)), pltpu.SemaphoreType.DMA((NCH,))]
    scratch += [pltpu.SemaphoreType.DMA((NCH + 1,))]
    grad, final = pl.pallas_call(
        kernel,
        out_shape=(
            jax.ShapeDtypeStruct((4, ROWS, LANES), F32),
            jax.ShapeDtypeStruct((1, ROWS, PLANE), BF16),
        ),
        in_specs=[hbm] * 9,
        out_specs=(hbm, hbm),
        scratch_shapes=scratch,
        compiler_params=pltpu.CompilerParams(
            collective_id=0, has_side_effects=True, vmem_limit_bytes=VMEM_LIMIT
        ),
    )(tile_slot, tile_list.T, q_model, rec_index, traces, adj_now, adj_prev, fwd_lap, mats)
    return pl.pallas_call(
        hand_over,
        out_shape=(
            jax.ShapeDtypeStruct(grad.shape, F32),
            jax.ShapeDtypeStruct(final.shape, BF16),
        ),
        in_specs=[vmem, vmem],
        out_specs=(vmem, vmem),
    )(grad, final)


def solution(mesh):
    in_specs = (
        P("shot", "sub", None),
        P(),
        P(),
        P("shot", None),
        P("shot", None, None),
        P("shot", "sub", None),
        P("shot", "sub", None),
        P("shot", None, "sub", None),
    )
    out_specs = (P("shot", "sub", None), P("shot", "sub", None))
    return jax.shard_map(body, mesh=mesh, in_specs=in_specs, out_specs=out_specs, check_vma=False)
```

```python
import jax
import jax.numpy as jnp
import numpy as np
from jax import lax
from jax.experimental import pallas as pl
from jax.experimental.pallas import tpu as pltpu
from jax.sharding import PartitionSpec as P

TS = 16
STEPS = 8
ROWS = 32
LANES = 256
PLANE = 4096
COEFFS = (-205.0 / 72.0, 8.0 / 5.0, -1.0 / 5.0, 8.0 / 315.0, -1.0 / 560.0)
C1 = COEFFS[1]
REL = tuple(c / C1 for c in COEFFS)

NCH = 4
R = ROWS // NCH
HC = 8
CB = 32 // HC

MESH = pl.DeviceIdType.MESH
VMEM_LIMIT = 60 * 1024 * 1024
F32 = jnp.float32
BF16 = jnp.bfloat16
DIRS = ((0, 1), (1, -1))


def lateral_matrices():
    out = np.zeros((3, LANES, LANES), np.float32)
    k = np.arange(LANES)[:, None]
    n = np.arange(LANES)[None, :]
    for d in (-1, 0, 1):
        dx = 4 * d + k // 64 - n // 64
        dy = k % 64 - n % 64
        for reach in range(1, 5):
            hit = ((dx == 0) & (np.abs(dy) == reach)) | ((dy == 0) & (np.abs(dx) == reach))
            out[d + 1][hit] = REL[reach]
    return np.concatenate([out, out]).reshape(6 * LANES, LANES)


def shot_at(y, x, z):
    return (y * 4 + x) * 4 + z


def ring(v):
    return (v + 8) & 3


class Links:
    def __init__(self):
        me = lax.axis_index("shot")
        self.at = {"y": me >> 4, "x": (me >> 2) & 3, "z": me & 3}
        self.shot = me
        self.sub = lax.axis_index("sub")

    def step(self, axis, delta):
        at = dict(self.at)
        at[axis] = ring(at[axis] + delta)
        return shot_at(at["y"], at["x"], at["z"])

    def copy(self, axis, delta, src, dst, sems, c, k):
        return pltpu.make_async_remote_copy(
            src_ref=src,
            dst_ref=dst,
            send_sem=sems[0].at[c, k],
            recv_sem=sems[1].at[c, k],
            device_id=(self.step(axis, delta), self.sub),
            device_id_type=MESH,
        )


def axes_of(c):
    return ("x", "y") if c % 2 == 0 else ("y", "x")


def slot_parts(slot, order):
    if order == 0:
        return slot >> 6, slot & 63
    return (slot >> 4) & 3, ((slot >> 6) << 4) + (slot & 15)


class Gather:
    def __init__(self, links, ts, tl, where, q_ref, QF, g, rel_s, rel_r, blk_s, blk_r, own_sem, sems):
        self.links, self.ts, self.tl, self.q_ref, self.QF = links, ts, tl, q_ref, QF
        self.g, self.rel_s, self.rel_r, self.blk_s, self.blk_r = g, rel_s, rel_r, blk_s, blk_r
        self.own_sem = own_sem
        self.where = where
        self.kept = {}
        self.sems = sems
        self.sent = []
        self.live = {}

    def go(self, name, c, d, axis, delta, src, dst, k):
        copy = self.links.copy(axis, delta, src, dst, self.sems, c, k + d)
        copy.start()
        self.sent.append(copy)
        self.live[name, c, d] = copy

    def got(self, name, c, d):
        self.live[name, c, d].wait_recv()

    def line(self, c):
        return self.links.at[axes_of(c)[0]]

    def part(self, c, line, zz, t0=0, n=4):
        return self.g[c].at[pl.ds(line * 16 + zz * 4 + t0, n)]

    def start(self, c):
        self.kept[c].wait()
        piece = self.part(c, self.line(c), self.links.at["z"])
        for d, delta in DIRS:
            self.go("zp1", c, d, "z", delta, piece, piece, 0)

    def own(self, c):
        self.spread("a1own", c, self.links.at["z"], 4)

    def keep(self, c):
        z, line = self.links.at["z"], self.line(c)
        copy = pltpu.make_async_copy(
            self.q_ref.at[:, pl.ds(c * R, R)], self.part(c, line, z), self.own_sem.at[c]
        )
        copy.start()
        self.kept[c] = copy

    def zp2(self, c):
        z, line = self.links.at["z"], self.line(c)
        for d, delta in DIRS:
            self.got("zp1", c, d)
            piece = self.part(c, line, ring(z - delta), 2 * d, 2)
            self.go("zp2", c, d, "z", delta, piece, piece, 2)

    def spread(self, name, c, zz, k):
        piece = self.part(c, self.line(c), zz)
        for d, delta in DIRS:
            self.go(name, c, d, axes_of(c)[0], delta, piece, piece, k)

    def a1n(self, c):
        z = self.links.at["z"]
        self.spread("a1m", c, ring(z - 1), 6)
        self.spread("a1p", c, ring(z + 1), 8)

    def a1f(self, c):
        for d in range(2):
            self.got("zp2", c, d)
        self.spread("a1f", c, ring(self.links.at["z"] + 2), 10)

    def forward(self, come, name, c, zz, k):
        for d, delta in DIRS:
            self.got(come, c, d)
            piece = self.part(c, ring(self.line(c) - delta), zz, 2 * d, 2)
            self.go(name, c, d, axes_of(c)[0], delta, piece, piece, k)

    def a2own(self, c):
        self.forward("a1own", "a2own", c, self.links.at["z"], 12)

    def a2n(self, c):
        z = self.links.at["z"]
        self.forward("a1m", "a2m", c, ring(z - 1), 14)
        self.forward("a1p", "a2p", c, ring(z + 1), 16)

    def a2f(self, c):
        self.forward("a1f", "a2f", c, ring(self.links.at["z"] + 2), 18)

    def target(self, c, delta, p):
        both = self.where[(c % 2) * 4 + delta % 4, p]
        return both >> 6, both & 63

    def targets(self):
        def fill(p, carry):
            for order in range(2):
                for delta in range(4):
                    slot = self.ts[self.tl[p, self.links.step(("y", "x")[order], delta)]]
                    owner, at = slot_parts(slot, order)
                    self.where[order * 4 + delta, p] = (owner << 6) + at
            return carry

        lax.fori_loop(0, 16, fill, 0)

    def rel(self, c):
        last = axes_of(c)[1]
        for d in range(2):
            for name in ("a2own", "a2m", "a2p", "a2f"):
                self.got(name, c, d)
        for d, delta in DIRS:
            for p in range(8):
                _, at = self.target(c, 2, 8 * d + p)
                self.rel_s[c][d, p] = self.g[c][at]
            self.go("rel", c, d, last, delta, self.rel_s[c].at[d], self.rel_r[c].at[d], 20)

    def half(self, name, c, d, delta, side, k):
        piece = pl.ds(8 * side, 8)
        self.go(
            name, c, d, axes_of(c)[1], delta,
            self.blk_s[c].at[d, piece], self.blk_r[c].at[d, piece], k,
        )

    def near(self, c):
        for d, delta in DIRS:
            for p in range(8 * (1 - d), 8 * (2 - d)):
                _, at = self.target(c, delta, p)
                self.blk_s[c][d, p] = self.g[c][at]
            self.half("near", c, d, delta, 1 - d, 24)

    def blk(self, c):
        mine = self.links.at[axes_of(c)[1]]
        for d, delta in DIRS:
            self.got("rel", c, d)
            for p in range(8 * d, 8 * (1 + d)):
                owner, at = self.target(c, delta, p)
                self.blk_s[c][d, p] = jnp.where(
                    owner == mine, self.g[c][at], self.rel_r[c][d, p % 8]
                )
            self.half("blk", c, d, delta, d, 22)

    def finish(self, c):
        mine = self.links.at[axes_of(c)[1]]
        blk_r = self.blk_r[c]
        for d in range(2):
            self.got("near", c, d)
            self.got("blk", c, d)
        for p in range(16):
            owner, at = self.target(c, 0, p)
            gap = ring(owner - mine)
            if p < 8:
                other = jnp.where(gap == 1, blk_r[1, p], blk_r[0, p])
            else:
                other = jnp.where(gap == 3, blk_r[0, p], blk_r[1, p])
            value = C1 * jnp.where(gap == 0, self.g[c][at], other)
            a, b = p // 4, p % 4
            for h in range(2):
                row = 32 * (2 * a + h) + c * R
                self.QF[row : row + R, 128 * b : 128 * b + 128] = value[:, 128 * h : 128 * h + 128]

    def drain(self):
        for copy in self.sent:
            copy.wait_send()


class Scatter:
    def __init__(
        self, links, tab, out_ref, GO, out_sem, gg, rel_s, rel_r, blk_s, blk_r, col, zrel_r, zblk_s, zblk_r, sems
    ):
        self.links, self.tab, self.out_ref, self.gg, self.col = links, tab, out_ref, gg, col
        self.rel_s, self.rel_r, self.blk_s, self.blk_r = rel_s, rel_r, blk_s, blk_r
        self.zrel_r, self.zblk_s, self.zblk_r = zrel_r, zblk_s, zblk_r
        self.GO, self.out_sem, self.outs = GO, out_sem, []
        self.sems = sems
        self.sent = []
        self.live = {}

    go = Gather.go
    got = Gather.got
    line = Gather.line
    drain = Gather.drain

    def first(self, c):
        return self.links.at[axes_of(c)[1]]

    def a1(self, c, half):
        for d, delta in DIRS:
            side = d if half == 0 else 1 - d
            piece = self.gg[c].at[pl.ds(self.first(c) * 16 + 8 * side, 8)]
            self.go(("a1", half), c, d, axes_of(c)[1], delta, piece, piece, 2 * half)

    def a2(self, c):
        for d, delta in DIRS:
            self.got(("a1", 0), c, d)
            piece = self.gg[c].at[pl.ds(ring(self.first(c) - delta) * 16 + 8 * d, 8)]
            self.go("a2", c, d, axes_of(c)[1], delta, piece, piece, 4)

    def partial(self, c, line, e):
        total = None
        for src in range(4):
            term = self.gg[c][self.tab[(c % 2) * 4 + src, line * 16 + e]]
            total = term if total is None else total + term
        return total

    def rel(self, c):
        for d in range(2):
            self.got(("a1", 1), c, d)
            self.got("a2", c, d)
        for d, delta in DIRS:
            for e in range(8):
                self.rel_s[c][d, e] = self.partial(c, ring(self.line(c) + 2), 8 * d + e)
            self.go(
                "rel", c, d, axes_of(c)[0], delta, self.rel_s[c].at[d], self.rel_r[c].at[d], 6
            )

    def own(self, c):
        for e in range(16):
            self.col[c][e] = self.partial(c, self.line(c), e)

    def half(self, name, c, d, delta, side, k):
        piece = pl.ds(8 * side, 8)
        self.go(
            name, c, d, axes_of(c)[0], delta,
            self.blk_s[c].at[d, piece], self.blk_r[c].at[d, piece], k,
        )

    def near(self, c):
        for d, delta in DIRS:
            for e in range(8 * (1 - d), 8 * (2 - d)):
                self.blk_s[c][d, e] = self.partial(c, ring(self.line(c) + delta), e)
            self.half("near", c, d, delta, 1 - d, 14)

    def blk(self, c):
        for d, delta in DIRS:
            self.got("rel", c, d)
            for e in range(8 * d, 8 * (1 + d)):
                value = self.partial(c, ring(self.line(c) + delta), e)
                self.blk_s[c][d, e] = value + self.rel_r[c][d, e % 8]
            self.half("blk", c, d, delta, d, 8)

    def zrel(self, c):
        z = self.links.at["z"]
        for d in range(2):
            self.got("near", c, d)
            self.got("blk", c, d)
        for e in range(16):
            self.col[c][e] += self.blk_r[c][0, e] + self.blk_r[c][1, e]
        for d, delta in DIRS:
            piece = self.col[c].at[pl.ds(ring(z + 2) * 4 + 2 * d, 2)]
            self.go("zrel", c, d, "z", delta, piece, self.zrel_r[c].at[d], 10)

    def znear(self, c):
        z = self.links.at["z"]
        for d, delta in DIRS:
            piece = self.col[c].at[pl.ds(ring(z + delta) * 4 + 2 * (1 - d), 2)]
            home = self.zblk_r[c].at[d, pl.ds(2 * (1 - d), 2)]
            self.go("znear", c, d, "z", delta, piece, home, 16)

    def zblk(self, c):
        z = self.links.at["z"]
        for d, delta in DIRS:
            self.got("zrel", c, d)
            for t in range(2):
                value = self.col[c][ring(z + delta) * 4 + 2 * d + t]
                self.zblk_s[c][d, t] = value + self.zrel_r[c][d, t]
            home = self.zblk_r[c].at[d, pl.ds(2 * d, 2)]
            self.go("zblk", c, d, "z", delta, self.zblk_s[c].at[d], home, 12)

    def finish(self, c):
        z = self.links.at["z"]
        for d in range(2):
            self.got("znear", c, d)
            self.got("zblk", c, d)
        for t in range(4):
            self.GO[c][t] = self.col[c][z * 4 + t] + self.zblk_r[c][0, t] + self.zblk_r[c][1, t]
        copy = pltpu.make_async_copy(
            self.GO[c], self.out_ref.at[:, pl.ds(c * R, R)], self.out_sem.at[c]
        )
        copy.start()
        self.outs.append(copy)


def split2(v):
    hi = v.astype(BF16)
    return hi, (v - hi.astype(F32)).astype(BF16)


def split3(v):
    hi = v.astype(BF16)
    rest = v - hi.astype(F32)
    mid = rest.astype(BF16)
    return hi, mid, (rest - mid.astype(F32)).astype(BF16)


def dot(a, b, transposed=False):
    dims = (((1,), (1,)), ((), ())) if transposed else (((1,), (0,)), ((), ()))
    return lax.dot_general(a, b, dims, preferred_element_type=F32)


def kernel(ts_hbm, tl_hbm, q_ref, rec_hbm, tr_hbm, u_hbm, w_hbm, fwd, mats_hbm, grad_out, fin_out, *scratch):
    scratch = list(scratch)

    def take(n):
        out = scratch[:n]
        del scratch[:n]
        return out

    U, H, LO, ACC, Q, G, S, PM, QF, T3, FW, hs, hr, tabv, tab, u_in, w_in, mats, FO, ts, tl, rec, tr, where = take(24)
    g, rel_s, rel_r, blk_s, blk_r = (take(NCH) for _ in range(5))
    gg, grel_s, grel_r, gblk_s, gblk_r = (take(NCH) for _ in range(5))
    col, zrel_r, zblk_s, zblk_r, GO = (take(NCH) for _ in range(5))
    ssem, rsem, qs, qr, gs, gr, lsem, own_sem, out_sem = take(9)

    links = Links()
    shot, sub = links.shot, links.sub
    has_up, has_dn = sub > 0, sub < 3
    sides = ((has_up, sub - 1), (has_dn, sub + 1))
    loads = [
        pltpu.make_async_copy(src, dst, lsem.at[k])
        for k, (src, dst) in enumerate(
            (
                (rec_hbm, rec), (tr_hbm, tr), (ts_hbm, ts), (tl_hbm, tl),
                (u_hbm, u_in), (w_hbm, w_in), (mats_hbm, mats), (fwd.at[0], FW),
            )
        )
    ]

    sem = pltpu.get_barrier_semaphore()
    for axis in ("y", "x", "z"):
        for delta in (1, -1):
            pl.semaphore_signal(
                sem, inc=1, device_id=(links.step(axis, delta), sub), device_id_type=MESH
            )
    for has, other in sides:

        @pl.when(has)
        def _():
            pl.semaphore_signal(sem, inc=1, device_id=(shot, other), device_id_type=MESH)

    gather = Gather(links, ts, tl, where, q_ref, QF, g, rel_s, rel_r, blk_s, blk_r, own_sem, (qs, qr))
    for c in range(NCH):
        gather.keep(c)
    for copy in loads:
        copy.start()

    def halo(slot, side, c):
        return pltpu.make_async_remote_copy(
            src_ref=hs.at[slot, side, c],
            dst_ref=hr.at[slot, 1 - side, c],
            send_sem=ssem.at[slot, side, c],
            recv_sem=rsem.at[slot, 1 - side, c],
            device_id=(shot, sides[side][1]),
            device_id_type=MESH,
        )

    def halo_in(slot, side, c):
        return pltpu.make_async_remote_copy(
            src_ref=hs.at[slot, side, c],
            dst_ref=hr.at[slot, side, c],
            send_sem=ssem.at[slot, side, c],
            recv_sem=rsem.at[slot, side, c],
            device_id=(shot, sides[side][1]),
            device_id_type=MESH,
        )

    def init_fields():
        zeros8 = jnp.zeros((32, 8, 128), F32)
        for par in range(2):
            U[par, :, 0:8, :] = zeros8
            U[par, :, 40:48, :] = zeros8
        for buf in (H, LO):
            buf[0:32, :] = jnp.zeros((32, LANES), BF16)
            buf[544:576, :] = jnp.zeros((32, LANES), BF16)
        for c in range(HC):
            for k in range(CB):
                cb = CB * c + k
                value = u_in[0, :, cb * 128 : (cb + 1) * 128]
                U[0, cb, 8:40, :] = value
                hs[0, 0, c, k] = value[0:4]
                hs[0, 1, c, k] = value[28:32]
                U[1, cb, 8:40, :] = w_in[0, :, cb * 128 : (cb + 1) * 128]
            for side in range(2):

                @pl.when(sides[side][0])
                def _():
                    halo(0, side, c).start()

        for j in range(16):
            hi, lo = split2(u_in[0, :, j * LANES : (j + 1) * LANES])
            H[32 + 32 * j : 64 + 32 * j, :] = hi
            LO[32 + 32 * j : 64 + 32 * j, :] = lo
        G[...] = jnp.zeros(G.shape, F32)
        tabv[...] = jnp.full((8, 128), 64, jnp.int32)
        for c in range(NCH):
            gg[c][64] = jnp.zeros((R, LANES), F32)

    loads[0].wait()
    loads[1].wait()
    receivers = rec[...]
    column = receivers & (PLANE - 1)
    level = (receivers >> 12) - sub * ROWS

    def source_values():
        depth_at = lax.broadcasted_iota(jnp.int32, (ROWS, LANES), 0)
        at_depth = depth_at == level
        for t in range(STEPS):
            value = jnp.where(at_depth, tr[0, t : t + 1, :], 0.0)
            for s, v in enumerate(split3(value)):
                T3[s, 32 * t : 32 * t + 32, 0:LANES] = v

    def source_block(j, carry):
        cell = lax.broadcasted_iota(jnp.int32, (LANES, LANES), 0)
        onehot = (cell + j * LANES == column).astype(F32).astype(BF16)
        total = dot(T3[0, :, 0:LANES], onehot, True)
        total = total + dot(T3[1, :, 0:LANES], onehot, True)
        total = total + dot(T3[2, :, 0:LANES], onehot, True)
        for t in range(STEPS):
            S[t, j] = total[32 * t : 32 * t + 32]
        return carry

    def sources(first, last):
        lax.fori_loop(first, last, source_block, 0)

    def permutation():
        src = lax.broadcasted_iota(jnp.int32, (512, 512), 0)
        dst = lax.broadcasted_iota(jnp.int32, (512, 512), 1)
        moved = ((src >> 4) & 7) * 64 + (src >> 7) * 16 + (src & 15)
        PM[...] = (moved == dst).astype(F32).astype(BF16)

    def lateral():
        wide = jnp.concatenate(
            [buf[32 * d : 32 * d + 512, :] for buf in (H, LO) for d in range(3)], axis=1
        )
        ACC[...] = dot(wide, mats[...])

    def table_rows(acc, p):
        row_at = lax.broadcasted_iota(jnp.int32, (8, 128), 0)
        lane_at = lax.broadcasted_iota(jnp.int32, (8, 128), 1)
        for order in range(2):
            first = ("y", "x")[order]
            m = links.at[first]
            for src in range(4):
                slot = ts[tl[p, links.step(first, src - m)]]
                owner, at = slot_parts(slot, order)
                at = jnp.where(owner == m, at, -1)
                hit = (row_at == order * 4 + src) & (lane_at == at)
                acc = jnp.where(hit, src * 16 + p, acc)
        return acc

    source_values()
    permutation()
    pl.semaphore_wait(sem, 6 + has_up.astype(jnp.int32) + has_dn.astype(jnp.int32))
    every = range(NCH)
    gather.start(0)
    gather.start(1)
    gather.own(0)
    gather.own(1)
    gather.start(2)
    gather.own(2)
    gather.start(3)
    gather.own(3)
    loads[2].wait()
    loads[3].wait()
    gather.targets()
    sources(0, 4)
    gather.zp2(0)
    gather.a2own(0)
    gather.a2own(1)
    gather.zp2(1)
    gather.a1n(1)
    gather.a1n(0)
    sources(4, 8)
    gather.zp2(2)
    loads[4].wait()
    loads[5].wait()
    init_fields()
    loads[6].wait()
    lateral()
    gather.a1n(2)
    gather.zp2(3)
    gather.a1n(3)
    sources(8, 12)
    gather.a1f(0)
    gather.a1f(1)
    gather.a2n(1)
    gather.a1f(2)
    gather.a2n(0)
    gather.a1f(3)
    gather.a2f(0)
    gather.a2f(1)
    gather.a2n(3)
    gather.a2own(3)
    gather.a2own(2)
    sources(12, 16)
    gather.a2f(2)
    gather.a2n(2)
    gather.a2f(3)
    gather.rel(0)
    gather.rel(1)
    gather.near(1)
    gather.near(0)
    gather.rel(2)
    gather.rel(3)
    gather.near(2)
    gather.near(3)
    gather.blk(0)
    gather.blk(1)
    gather.blk(2)
    gather.blk(3)
    gather.finish(0)
    gather.finish(1)
    gather.finish(2)
    gather.finish(3)
    loads[7].wait()
    gather.drain()

    for k in range(8):
        for s, v in enumerate(split2(QF[32 * k : 32 * k + 32, :])):
            T3[s, 32 * k : 32 * k + 32, :] = v
    for n in range(2):
        perm = PM[:, LANES * n : LANES * n + LANES]
        total = dot(T3[0], perm) + dot(T3[1], perm)
        for k in range(8):
            Q[2 * k + n] = total[32 * k : 32 * k + 32]

    def one_step(t, carry):
        par = lax.rem(t, 2)
        nxt = 1 - par
        for c in range(HC):
            for side in range(2):

                @pl.when(sides[side][0])
                def _():
                    halo(par, side, c).wait_send()
                    halo_in(par, side, c).wait_recv()
                    first = 4 if side == 0 else 40
                    for k in range(CB):
                        U[par, CB * c + k, first : first + 4, :] = hr[par, side, c, k]

            for jj in range(CB // 2):
                j = CB // 2 * c + jj
                half = []
                for h in range(2):
                    cb = 2 * j + h
                    here = U[par, cb, 8:40, :]
                    lanes = slice(128 * h, 128 * h + 128)
                    acc = (3.0 * REL[0]) * here + ACC[32 * j : 32 * j + 32, lanes]
                    for reach in range(1, 5):
                        beside = U[par, cb, 8 + reach : 40 + reach, :] + U[par, cb, 8 - reach : 40 - reach, :]
                        acc = acc + (beside if reach == 1 else REL[reach] * beside)
                    new = 2.0 * here - U[nxt, cb, 8:40, :] + Q[j, :, lanes] * acc + S[t, j, :, lanes]
                    U[nxt, cb, 8:40, :] = new
                    hs[nxt, 0, c, 2 * jj + h] = new[0:4]
                    hs[nxt, 1, c, 2 * jj + h] = new[28:32]
                    G[j, :, lanes] += FW[t, :, cb * 128 : cb * 128 + 128].astype(F32) * new
                    half.append(new)
                hi, lo = split2(jnp.concatenate(half, axis=1))
                H[32 + 32 * j : 64 + 32 * j, :] = hi
                LO[32 + 32 * j : 64 + 32 * j, :] = lo
            for side in range(2):

                @pl.when(sides[side][0] & (t < STEPS - 1))
                def _():
                    halo(nxt, side, c).start()

        pl.when(t < STEPS - 1)(lateral)
        tabv[...] = table_rows(table_rows(tabv[...], 2 * t), 2 * t + 1)
        return carry

    lax.fori_loop(0, STEPS, one_step, 0)
    fill = pltpu.make_async_copy(tabv, tab, lsem.at[8])
    fill.start()

    scatter = Scatter(
        links, tab, grad_out, GO, out_sem, gg, grel_s, grel_r, gblk_s, gblk_r, col, zrel_r, zblk_s, zblk_r, (gs, gr)
    )
    for k in range(8):
        wide = jnp.concatenate([G[2 * k], G[2 * k + 1]], axis=1)
        for s, v in enumerate(split2(wide)):
            T3[s, 32 * k : 32 * k + 32, :] = v
    for n in range(2):
        perm = PM[LANES * n : LANES * n + LANES, :]
        total = dot(T3[0], perm, True) + dot(T3[1], perm, True)
        for k in range(8):
            a, h = k // 2, k % 2
            for b in range(2):
                for c in range(NCH):
                    at = scatter.first(c) * 16 + 4 * a + 2 * n + b
                    row = 32 * k + c * R
                    gg[c][at, :, 128 * h : 128 * h + 128] = total[
                        row : row + R, 128 * b : 128 * b + 128
                    ]
    scatter.a1(1, 0)
    scatter.a1(0, 0)
    scatter.a1(2, 0)
    scatter.a1(3, 0)
    scatter.a1(3, 1)
    scatter.a1(0, 1)
    for cb in range(32):
        FO[0, :, cb * 128 : (cb + 1) * 128] = U[STEPS % 2, cb, 8:40, :].astype(BF16)
    final = pltpu.make_async_copy(FO, fin_out, out_sem.at[NCH])
    final.start()
    fill.wait()
    scatter.a2(0)
    scatter.a1(1, 1)
    scatter.a1(2, 1)
    scatter.a2(1)
    scatter.a2(3)
    scatter.a2(2)
    scatter.rel(0)
    scatter.rel(1)
    scatter.near(0)
    scatter.own(0)
    scatter.rel(3)
    scatter.rel(2)
    scatter.blk(0)
    scatter.near(1)
    scatter.near(2)
    scatter.blk(1)
    scatter.near(3)
    scatter.blk(3)
    scatter.blk(2)
    scatter.zrel(0)
    scatter.own(2)
    scatter.znear(0)
    scatter.own(1)
    scatter.own(3)
    scatter.zrel(1)
    scatter.znear(1)
    scatter.zrel(2)
    scatter.znear(2)
    scatter.zrel(3)
    scatter.zblk(0)
    scatter.zblk(1)
    scatter.znear(3)
    scatter.zblk(2)
    scatter.zblk(3)
    scatter.finish(2)
    scatter.finish(0)
    scatter.finish(1)
    scatter.finish(3)
    scatter.drain()
    final.wait()
    for copy in scatter.outs:
        copy.wait()


def hand_over(grad, final, grad_out, fin_out):
    grad_out[...] = grad[...]
    fin_out[...] = final[...]


def body(q_model, tile_slot, tile_list, rec_index, traces, adj_now, adj_prev, fwd_lap):
    vmem = pl.BlockSpec(memory_space=pltpu.VMEM)
    hbm = pl.BlockSpec(memory_space=pl.ANY)
    mats = jnp.asarray(lateral_matrices(), BF16)
    scratch = [
        pltpu.VMEM((2, 32, 48, 128), F32),
        pltpu.VMEM((576, LANES), BF16),
        pltpu.VMEM((576, LANES), BF16),
        pltpu.VMEM((512, LANES), F32),
        pltpu.VMEM((16, ROWS, LANES), F32),
        pltpu.VMEM((16, ROWS, LANES), F32),
        pltpu.VMEM((STEPS, 16, ROWS, LANES), F32),
        pltpu.VMEM((512, 512), BF16),
        pltpu.VMEM((256, 512), F32),
        pltpu.VMEM((3, 256, 512), BF16),
        pltpu.VMEM((STEPS, ROWS, PLANE), BF16),
        pltpu.VMEM((2, 2, HC, CB, 4, 128), F32),
        pltpu.VMEM((2, 2, HC, CB, 4, 128), F32),
        pltpu.VMEM((8, 128), jnp.int32),
        pltpu.SMEM((8, 128), jnp.int32),
        pltpu.VMEM((1, ROWS, PLANE), F32),
        pltpu.VMEM((1, ROWS, PLANE), F32),
        pltpu.VMEM((6 * LANES, LANES), BF16),
        pltpu.VMEM((1, ROWS, PLANE), BF16),
        pltpu.SMEM((256,), jnp.int32),
        pltpu.SMEM((16, 64), jnp.int32),
        pltpu.VMEM((1, LANES), jnp.int32),
        pltpu.VMEM((1, STEPS, LANES), F32),
        pltpu.SMEM((8, 16), jnp.int32),
    ]
    scratch += [pltpu.VMEM((64, R, LANES), F32)] * NCH
    scratch += [pltpu.VMEM((2, 8, R, LANES), F32)] * (2 * NCH)
    scratch += [pltpu.VMEM((2, 16, R, LANES), F32)] * (2 * NCH)
    scratch += [pltpu.VMEM((65, R, LANES), F32)] * NCH
    scratch += [pltpu.VMEM((2, 8, R, LANES), F32)] * (2 * NCH)
    scratch += [pltpu.VMEM((2, 16, R, LANES), F32)] * (2 * NCH)
    scratch += [pltpu.VMEM((16, R, LANES), F32)] * NCH
    scratch += [pltpu.VMEM((2, 2, R, LANES), F32)] * NCH
    scratch += [pltpu.VMEM((2, 2, R, LANES), F32)] * NCH
    scratch += [pltpu.VMEM((2, 4, R, LANES), F32)] * NCH
    scratch += [pltpu.VMEM((4, R, LANES), F32)] * NCH
    scratch += [pltpu.SemaphoreType.DMA((2, 2, HC))] * 2
    scratch += [pltpu.SemaphoreType.DMA((NCH, 26))] * 2
    scratch += [pltpu.SemaphoreType.DMA((NCH, 18))] * 2
    scratch += [pltpu.SemaphoreType.DMA((9,)), pltpu.SemaphoreType.DMA((NCH,))]
    scratch += [pltpu.SemaphoreType.DMA((NCH + 1,))]
    grad, final = pl.pallas_call(
        kernel,
        out_shape=(
            jax.ShapeDtypeStruct((4, ROWS, LANES), F32),
            jax.ShapeDtypeStruct((1, ROWS, PLANE), BF16),
        ),
        in_specs=[hbm] * 9,
        out_specs=(hbm, hbm),
        scratch_shapes=scratch,
        compiler_params=pltpu.CompilerParams(
            collective_id=0, has_side_effects=True, vmem_limit_bytes=VMEM_LIMIT
        ),
    )(tile_slot, tile_list.T, q_model, rec_index, traces, adj_now, adj_prev, fwd_lap, mats)
    return pl.pallas_call(
        hand_over,
        out_shape=(
            jax.ShapeDtypeStruct(grad.shape, F32),
            jax.ShapeDtypeStruct(final.shape, BF16),
        ),
        in_specs=[vmem, vmem],
        out_specs=(vmem, vmem),
    )(grad, final)


def solution(mesh):
    in_specs = (
        P("shot", "sub", None),
        P(),
        P(),
        P("shot", None),
        P("shot", None, None),
        P("shot", "sub", None),
        P("shot", "sub", None),
        P("shot", None, "sub", None),
    )
    out_specs = (P("shot", "sub", None), P("shot", "sub", None))
    return jax.shard_map(body, mesh=mesh, in_specs=in_specs, out_specs=out_specs, check_vma=False)
```
